256 devices in a mesh: ctx: 64 (over z_lo, x, y), rep: 4 (over z_hi, core).
Axes of the slice: x: 4, y: 4, z: 8 (z_hi: 2, z_lo: 4; z = z_hi * 4 + z_lo), core: 2. Of those that a mesh axis runs over, the one named last changes fastest.
Arguments:
- inputs: bfloat16 [4, 16384, 256], P('rep', 'ctx'), may hold values from -6 to 6
- w_expand: bfloat16 [512, 1024], replicated, may hold values from -0.25 to 0.25
- b_expand: float32 [1024], replicated, may hold values from -1 to 1
- w_reduce: bfloat16 [1024, 512], replicated, may hold values from -0.1875 to 0.1875
- b_reduce: float32 [512], replicated, may hold values from -0.5 to 0.5
- gate_logit: float32 [512], replicated, may hold values from -2 to 2
- cotangent: bfloat16 [4, 16384, 256], P('rep', 'ctx'), may hold values from -6 to 6
Outputs:
- outputs: bfloat16 [4, 16384, 256], P('rep', 'ctx')
- grad_inputs: bfloat16 [4, 16384, 256], P('rep', 'ctx')
- grad_w_expand: float32 [512, 1024], P('ctx')
- grad_b_expand: float32 [1024], replicated
- grad_w_reduce: float32 [1024, 512], P('ctx')
- grad_b_reduce: float32 [512], replicated
- grad_gate: float32 [512], replicated
The draws below stay inside these ranges and needn't reach their ends.
All inputs are finite; a program needn't handle non-finite values.
Results may differ from the reference program's by a relative error of at most 0.018.
Values may be sent and summed in bfloat16 or wider, within the bound.
A program may use at most 64 MiB of HBM per device.

```python
import math
import jax
import jax.numpy as jnp
from jax import lax

M = 256
H = 1024
P_DEV = 256
SECTIONS = 4
SEQS = 4
LENGTH = 16384
N_CTX = 64


def level_of(key, dims, cuts, least, high):
    def one(dim, blocks):
        steps = jax.random.uniform(jax.random.fold_in(jax.random.fold_in(key, 6), dim), (blocks,), jnp.float32, least / len(cuts), high / len(cuts))
        return jnp.repeat(jnp.exp(steps), dims[dim] // blocks).reshape((-1,) + (1,) * (len(dims) - dim - 1))

    level = one(*cuts[0])
    for cut in cuts[1:]:
        level = level * one(*cut)
    return level


def gaussian(rng, dims, deviation, reach, split=(), kind=jnp.bfloat16):
    entries = deviation * jax.random.normal(rng, dims, jnp.float32)
    if split:
        entries = entries * level_of(rng, dims, split, -0.22, 0.18)
    return jnp.clip(entries, -reach, reach).astype(kind)


def setup_inputs(seed: int = 0) -> dict:
    splits = jax.random.split(jax.random.key(seed), 8)
    inputs = gaussian(splits[0], (SEQS, LENGTH, M), 1.0, 6.0, ((0, 4), (1, 64)))
    w_expand = gaussian(splits[1], (2 * M, H), (2 * M) ** -0.5, 0.25)
    b_expand = jnp.clip(jax.random.uniform(splits[2], (H,), jnp.float32, -1.0, 1.0), -1.0, 1.0)
    w_reduce = gaussian(splits[3], (H, 2 * M), H ** -0.5, 0.1875)
    b_reduce = jnp.clip(jax.random.uniform(splits[4], (2 * M,), jnp.float32, -0.5, 0.5), -0.5, 0.5)
    gate_logit = jnp.clip(jax.random.uniform(splits[5], (2 * M,), jnp.float32, -2.0, 2.0), -2.0, 2.0)
    cotangent = gaussian(splits[6], (SEQS, LENGTH, M), 1.0, 6.0, ((0, 4), (1, 64)))
    return dict(inputs=inputs, w_expand=w_expand, b_expand=b_expand, w_reduce=w_reduce, b_reduce=b_reduce, gate_logit=gate_logit, cotangent=cotangent)


EPSILON = 1e-05

def gelu_back(preact, upstream):
    return jax.vjp(lambda value: jax.nn.gelu(value, approximate=False), preact)[1](upstream)[0]

def switch_forward(lower, upper, w_expand, b_expand):
    joined = jnp.concatenate([lower, upper], axis=-1).astype(jnp.float32)
    centred = joined - lax.optimization_barrier(jnp.mean(joined, axis=-1, keepdims=True))
    inv_std = lax.rsqrt(lax.optimization_barrier(jnp.mean(centred * centred, axis=-1, keepdims=True)) + EPSILON)
    normed = centred * inv_std
    normed_low = normed.astype(jnp.bfloat16)
    preact = jnp.dot(normed_low, w_expand, preferred_element_type=jnp.float32) + b_expand
    hidden = jax.nn.gelu(preact, approximate=False).astype(jnp.bfloat16)
    return (joined, normed, inv_std, normed_low, preact, hidden)

def switch_apply(lower, upper, w_expand, b_expand, w_reduce, b_reduce, gate_logit):
    joined, normed, inv_std, normed_low, preact, hidden = switch_forward(lower, upper, w_expand, b_expand)
    mixed = jnp.dot(hidden, w_reduce, preferred_element_type=jnp.float32)
    result = (jax.nn.sigmoid(gate_logit) * joined + mixed + b_reduce).astype(jnp.bfloat16)
    width = lower.shape[-1]
    return (result[:, :width], result[:, width:])

def switch_backward(lower, upper, grad_lower, grad_upper, w_expand, b_expand, w_reduce, b_reduce, gate_logit):
    joined, normed, inv_std, normed_low, preact, hidden = switch_forward(lower, upper, w_expand, b_expand)
    grad_out = jnp.concatenate([grad_lower, grad_upper], axis=-1)
    grad_float = grad_out.astype(jnp.float32)
    sigma = jax.nn.sigmoid(gate_logit)
    grad_bias_red = lax.optimization_barrier(jnp.sum(grad_float, axis=0))
    grad_gate = lax.optimization_barrier(jnp.sum(grad_float * joined, axis=0)) * sigma * (1.0 - sigma)
    grad_weight_red = jnp.dot(hidden.T, grad_out, preferred_element_type=jnp.float32)
    grad_hidden = jnp.dot(grad_out, w_reduce.T, preferred_element_type=jnp.float32)
    grad_pre = gelu_back(preact, grad_hidden)
    grad_pre_low = grad_pre.astype(jnp.bfloat16)
    grad_bias_exp = lax.optimization_barrier(jnp.sum(grad_pre, axis=0))
    grad_weight_exp = jnp.dot(normed_low.T, grad_pre_low, preferred_element_type=jnp.float32)
    grad_normed = jnp.dot(grad_pre_low, w_expand.T, preferred_element_type=jnp.float32)
    grad_joined = sigma * grad_float + inv_std * (grad_normed - lax.optimization_barrier(jnp.mean(grad_normed, axis=-1, keepdims=True)) - normed * lax.optimization_barrier(jnp.mean(grad_normed * normed, axis=-1, keepdims=True)))
    grad_joined = grad_joined.astype(jnp.bfloat16)
    width = lower.shape[-1]
    return (grad_joined[:, :width], grad_joined[:, width:], (grad_weight_exp, grad_bias_exp, grad_weight_red, grad_bias_red, grad_gate))

def split_pairs(state, block):
    seqs, length, width = state.shape
    groups = length // (2 * block)
    view = state.reshape(seqs, groups, 2, block, width)
    return (view[:, :, 0].reshape(-1, width), view[:, :, 1].reshape(-1, width))

def join_pairs(first, second, shape, block):
    seqs, length, width = shape
    groups = length // (2 * block)
    return jnp.stack([first.reshape(seqs, groups, block, width), second.reshape(seqs, groups, block, width)], axis=2).reshape(seqs, length, width)

def reference(inputs, w_expand, b_expand, w_reduce, b_reduce, gate_logit, cotangent):
    weights = (w_expand, b_expand, w_reduce, b_reduce, gate_logit)
    count = N_CTX.bit_length() - 1
    bits = [(count - 1 - section) % count for section in range(SECTIONS)]
    shape = inputs.shape
    state = inputs
    saved = []
    for bit in bits:
        block = P_DEV * 2 ** bit
        lower, upper = split_pairs(state, block)
        saved.append((lower, upper))
        out_lower, out_upper = switch_apply(lower, upper, *weights)
        state = join_pairs(out_lower, out_upper, shape, block)
    outputs = state
    grad_state = cotangent
    totals = (jnp.zeros(w_expand.shape, jnp.float32), jnp.zeros(b_expand.shape, jnp.float32), jnp.zeros(w_reduce.shape, jnp.float32), jnp.zeros(b_reduce.shape, jnp.float32), jnp.zeros(gate_logit.shape, jnp.float32))
    for section in reversed(range(SECTIONS)):
        block = P_DEV * 2 ** bits[section]
        lower, upper = saved[section]
        grad_lower, grad_upper = split_pairs(grad_state, block)
        back_lower, back_upper, grads = switch_backward(lower, upper, grad_lower, grad_upper, *weights)
        totals = tuple((total + piece for total, piece in zip(totals, grads)))
        grad_state = join_pairs(back_lower, back_upper, shape, block)
    factor = 1.0 / math.sqrt(shape[0] * shape[1])
    return (outputs, grad_state, totals[0] * factor, totals[1] * factor, totals[2] * factor, totals[3] * factor, totals[4] * factor)
```

```python
import functools
import math

import jax
import jax.numpy as jnp
from jax import lax
from jax.experimental import pallas as pl
from jax.experimental.pallas import tpu as pltpu
from jax.sharding import PartitionSpec as P

MESH = pl.DeviceIdType.MESH
F32 = jnp.float32
BF16 = jnp.bfloat16
EPSILON = 1e-05
SECTIONS = 4
GROUP = 16


def dot(a, b, dims):
    return lax.dot_general(a, b, (dims, ((), ())), preferred_element_type=F32)


NN = ((1,), (0,))
NT = ((1,), (1,))


def kernel(
    factor,
    x_ref,
    we_hbm,
    be_ref,
    wr_hbm,
    br_ref,
    gl_ref,
    ct_ref,
    out_ref,
    gin_ref,
    o_we,
    o_be,
    o_wr,
    o_br,
    o_gg,
    we,
    wr,
    st,
    gst,
    nrm,
    inv,
    norm_t,
    hid_t,
    dgelu,
    gout,
    gpre,
    own,
    sib,
    rsib,
    part,
    recv1,
    mid,
    recv2,
    zsend,
    zrecv,
    fin,
    rfin,
    acc_be,
    acc_br,
    acc_gg,
    vec,
    rvec,
    vx,
    vy,
    vz,
    load_sem,
    a_send,
    a_recv,
    c_send,
    c_recv,
    p_send,
    p_recv,
    q_send,
    q_recv,
    z_send,
    z_recv,
    b_send,
    b_recv,
):
    ctx = lax.axis_index("ctx")
    rep = lax.axis_index("rep")
    y = lax.rem(ctx, 4)
    member = lax.div(ctx, 4)
    x = lax.rem(member, 4)
    z_lo = lax.div(member, 4)
    core = lax.rem(rep, 2)
    z_hi = lax.div(rep, 2)
    z = z_hi * 4 + z_lo

    def at_member(m):
        return (m * 4 + y, rep)

    def at_x(v):
        return (z_lo * 16 + v * 4 + y, rep)

    def at_y(v):
        return (member * 4 + v, rep)

    def at_z(v):
        return (lax.rem(v, 4) * 16 + x * 4 + y, lax.div(v, 4) * 2 + core)

    sibling = (ctx, z_hi * 2 + 1 - core)

    def remote(src, dst, send, recv, device):
        return pltpu.make_async_remote_copy(
            src_ref=src, dst_ref=dst, send_sem=send, recv_sem=recv, device_id=device, device_id_type=MESH
        )

    load_we = pltpu.make_async_copy(we_hbm, we, load_sem.at[0])
    load_wr = pltpu.make_async_copy(wr_hbm, wr, load_sem.at[1])
    own_x = pltpu.make_async_copy(x_ref.at[member], st.at[0, member], load_sem.at[2])
    own_ct = pltpu.make_async_copy(ct_ref.at[member], gst.at[SECTIONS, member], load_sem.at[3])
    own_x.start()
    load_we.start()
    load_wr.start()
    own_ct.start()

    barrier = pltpu.get_barrier_semaphore()

    def hello(device):
        pl.semaphore_signal(barrier, inc=1, device_id=device, device_id_type=MESH)

    @pl.loop(1, GROUP)
    def _(o):
        hello(at_member(lax.rem(member + o, GROUP)))

    for o in range(1, 4):
        hello(at_y(lax.rem(y + o, 4)))
    for v in range(4):
        hello(at_z((1 - z_hi) * 4 + v))
    hello(sibling)
    pl.semaphore_wait(barrier, 23)

    def exchange(kind, src, dst):
        def copy(o):
            m = lax.rem(member + o, GROUP)
            return remote(src.at[m], dst.at[member], a_send.at[kind, o], a_recv.at[kind, o], at_member(m))

        def start():
            @pl.loop(1, GROUP)
            def _(o):
                copy(o).start()

        def arrive():
            @pl.loop(1, GROUP)
            def _(o):
                m = lax.rem(member + GROUP - o, GROUP)
                remote(src.at[m], dst.at[m], a_send.at[kind, o], a_recv.at[kind, o], at_member(m)).wait_recv()

        def sent():
            @pl.loop(1, GROUP)
            def _(o):
                copy(o).wait_send()

        return start, arrive, sent

    in_start, in_arrive, in_sent = exchange(0, x_ref, st.at[0])
    ct_start, ct_arrive, ct_sent = exchange(1, ct_ref, gst.at[SECTIONS])
    out_start, out_arrive, out_sent = exchange(2, st.at[SECTIONS], out_ref)
    gin_start, gin_arrive, gin_sent = exchange(3, gst.at[0], gin_ref)
    in_start()
    ct_start()

    acc_be[...] = jnp.zeros_like(acc_be)
    acc_br[...] = jnp.zeros_like(acc_br)
    acc_gg[...] = jnp.zeros_like(acc_gg)
    sigma = jax.nn.sigmoid(gl_ref[...])

    load_we.wait()
    load_wr.wait()
    own_x.wait()
    in_arrive()

    def joined_of(s):
        lower = st[s, 0:8].reshape(128, 256).astype(F32)
        upper = st[s, 8:16].reshape(128, 256).astype(F32)
        return jnp.concatenate([lower, upper], axis=1)

    def forward(s):
        cols = pl.ds(pl.multiple_of(s * 128, 128), 128)
        joined = joined_of(s)
        centred = joined - jnp.mean(joined, axis=1, keepdims=True)
        inv_std = lax.rsqrt(jnp.mean(centred * centred, axis=1, keepdims=True) + EPSILON)
        normed = centred * inv_std
        nrm[s] = normed
        inv[s] = inv_std
        low = normed.astype(BF16)
        norm_t[:, cols] = low.T
        mixed = sigma * joined + br_ref[...]
        for h in range(4):
            hs = slice(256 * h, 256 * h + 256)
            pre = dot(low, we[:, hs], NN) + be_ref[:, hs]
            cdf = 0.5 + 0.5 * lax.erf(pre * math.sqrt(0.5))
            pdf = jnp.exp(-0.5 * pre * pre) * (1.0 / math.sqrt(2.0 * math.pi))
            dgelu[s, :, hs] = cdf + pre * pdf
            hidden = (pre * cdf).astype(BF16)
            hid_t[hs, cols] = hidden.T
            mixed = mixed + dot(hidden, wr[hs, :], NN)
        result = mixed.astype(BF16)
        for j in range(8):
            st[s + 1, 2 * j] = result[16 * j : 16 * j + 16, :256]
            st[s + 1, 2 * j + 1] = result[16 * j : 16 * j + 16, 256:]

    @pl.loop(0, SECTIONS)
    def _(s):
        forward(s)

    out_start()
    own_out = pltpu.make_async_copy(st.at[SECTIONS, member], out_ref.at[member], load_sem.at[4])
    own_out.start()

    own_ct.wait()
    ct_arrive()

    def rows_of(s):
        return pl.ds(pl.multiple_of(s * 128, 128), 128)

    def upstream(s):
        lower = jnp.concatenate([gst[s + 1, 2 * j] for j in range(8)], axis=0)
        upper = jnp.concatenate([gst[s + 1, 2 * j + 1] for j in range(8)], axis=0)
        gout[rows_of(s), :] = jnp.concatenate([lower, upper], axis=1)

    def fold(v):
        return jnp.sum(v.reshape(16, 8, v.shape[1]), axis=0)

    def backward(s):
        grad = gout[rows_of(s), :]
        wide = grad.astype(F32)
        acc_br[...] += fold(wide)
        acc_gg[...] += fold(wide * joined_of(s))
        gnormed = None
        for h in range(4):
            hs = slice(256 * h, 256 * h + 256)
            pre = dot(grad, wr[hs, :], NT) * dgelu[s, :, hs]
            acc_be[:, hs] += fold(pre)
            low = pre.astype(BF16)
            gpre[rows_of(s), hs] = low
            term = dot(low, we[:, hs], NT)
            gnormed = term if gnormed is None else gnormed + term
        normed = nrm[s]
        mean = jnp.mean(gnormed, axis=1, keepdims=True)
        along = jnp.mean(gnormed * normed, axis=1, keepdims=True)
        result = (sigma * wide + inv[s] * (gnormed - mean - normed * along)).astype(BF16)
        gst[s, 0:8] = result[:, :256].reshape(8, 16, 256)
        gst[s, 8:16] = result[:, 256:].reshape(8, 16, 256)

    def core_copy(k):
        return remote(sib.at[k], rsib.at[k], c_send.at[k], c_recv.at[k], sibling)

    def gradient(k, mine):
        who = core if mine else 1 - core
        if k < 2:
            left = hid_t[512 * k : 512 * k + 512, :]
            right = gout[:, pl.ds(pl.multiple_of(256 * who, 256), 256)]
            blocks = dot(left, right, NN).reshape(2, 16, 16, 256)
        else:
            left = norm_t[...]
            right = gpre[:, pl.ds(pl.multiple_of(512 * who + 256 * (k - 2), 256), 256)]
            blocks = dot(left, right, NN).reshape(4, 16, 8, 256)
        value = jnp.concatenate([blocks[i] for i in range(blocks.shape[0])], axis=1)
        if mine:
            own[k] = value
        else:
            sib[k] = value.astype(BF16)

    def make(k):
        gradient(k, False)
        core_copy(k).start()
        gradient(k, True)

    x_first = (True, False, True, False)

    def first(k, o, to):
        if x_first[k]:
            v = lax.rem(x + o, 4)
            src = part.at[k, v]
            device = at_x(v)
        else:
            v = lax.rem(y + o, 4)
            src = part.at[k, :, v]
            device = at_y(v)
        return remote(src, recv1.at[k, o], p_send.at[k, o], p_recv.at[k, o], device)

    def second(k, o):
        if x_first[k]:
            v = lax.rem(y + o, 4)
            device = at_y(v)
        else:
            v = lax.rem(x + o, 4)
            device = at_x(v)
        return remote(mid.at[k, v], recv2.at[k, o], q_send.at[k, o], q_recv.at[k, o], device)

    def scatter(k):
        core_copy(k).wait_recv()
        total = own[k] + rsib[k].astype(F32)
        part[k] = total.astype(BF16).reshape(4, 4, 32, 256)
        for o in range(1, 4):
            first(k, o, True).start()

    def scatter_again(k):
        for o in range(1, 4):
            first(k, o, False).wait_recv()
        mine = part[k, x] if x_first[k] else part[k, :, y]
        total = mine.astype(F32)
        for o in range(1, 4):
            total = total + recv1[k, o].astype(F32)
        mid[k] = total.astype(BF16)
        for o in range(1, 4):
            second(k, o).start()

    def reduced(k):
        for o in range(1, 4):
            second(k, o).wait_recv()
        total = (mid[k, y] if x_first[k] else mid[k, x]).astype(F32)
        for o in range(1, 4):
            total = total + recv2[k, o].astype(F32)
        return total

    def z_copy(o):
        v = lax.rem(z + o, 8)
        return remote(zsend.at[lax.rem(v, 4)], zrecv.at[z], z_send.at[o], z_recv.at[o], at_z(v))

    def z_arrive(o):
        v = lax.rem(z + 8 - o, 8)
        remote(zsend.at[0], zrecv.at[v], z_send.at[o], z_recv.at[o], at_z(v)).wait_recv()

    def b_copy(n, o):
        sems = (b_send.at[n, o], b_recv.at[n, o])
        if n == 0:
            return remote(vec, rvec, *sems, sibling)
        if n == 1:
            return remote(vx.at[x], vx.at[x], *sems, at_x(lax.rem(x + o, 4)))
        if n == 2:
            return remote(vy.at[y], vy.at[y], *sems, at_y(lax.rem(y + o, 4)))
        return remote(vz.at[z], vz.at[z], *sems, at_z(lax.rem(z + o, 8)))

    def b_arrive(n, o):
        sems = (b_send.at[n, o], b_recv.at[n, o])
        if n == 0:
            remote(vec, rvec, *sems, sibling).wait_recv()
        elif n == 1:
            v = lax.rem(x + 4 - o, 4)
            remote(vx.at[v], vx.at[v], *sems, at_x(v)).wait_recv()
        elif n == 2:
            v = lax.rem(y + 4 - o, 4)
            remote(vy.at[v], vy.at[v], *sems, at_y(v)).wait_recv()
        else:
            v = lax.rem(z + 8 - o, 8)
            remote(vz.at[v], vz.at[v], *sems, at_z(v)).wait_recv()

    B_COUNT = (range(0, 1), range(1, 4), range(1, 4), range(1, 8))

    def b_begin(n):
        for o in B_COUNT[n]:
            b_copy(n, o).start()

    def b_end(n):
        for o in B_COUNT[n]:
            b_arrive(n, o)

    @pl.loop(0, SECTIONS - 1)
    def _(i):
        s = SECTIONS - 1 - i
        upstream(s)
        backward(s)

    upstream(0)
    make(0)
    make(1)
    scatter(0)
    backward(0)
    gin_start()
    own_gin = pltpu.make_async_copy(gst.at[0, member], gin_ref.at[member], load_sem.at[5])
    own_gin.start()
    scatter(1)
    make(2)
    make(3)

    def put(row, v):
        total = jnp.sum(v, axis=0, keepdims=True)
        for i in range(v.shape[1] // 256):
            vec[row + i : row + i + 1, :] = total[:, 256 * i : 256 * i + 256]

    put(0, acc_be[...])
    put(4, acc_br[...])
    put(6, acc_gg[...])
    b_begin(0)
    scatter(2)
    scatter_again(0)
    scatter(3)
    scatter_again(1)
    b_end(0)
    vx[x] = vec[...] + rvec[...]
    b_begin(1)
    f0 = reduced(0)
    f1 = reduced(1)
    for i in range(2):
        zsend[i, 0:16] = f0[16 * i : 16 * i + 16].astype(BF16)
        zsend[2 + i, 0:16] = f1[16 * i : 16 * i + 16].astype(BF16)
    scatter_again(2)
    scatter_again(3)
    b_end(1)
    vy[y] = (vx[0] + vx[1]) + (vx[2] + vx[3])
    b_begin(2)
    f2 = reduced(2)
    f3 = reduced(3)
    for i in range(4):
        rows = slice(8 * i, 8 * i + 8)
        zsend[i, 16:32] = jnp.concatenate([f2[rows], f3[rows]], axis=0).astype(BF16)
    for o in range(1, 8):
        z_copy(o).start()
    b_end(2)
    vz[z] = (vy[0] + vy[1]) + (vy[2] + vy[3])
    b_begin(3)
    zrecv[z] = zsend[z_lo]
    for o in range(1, 8):
        z_arrive(o)
    total = zrecv[0].astype(F32)
    for v in range(1, 8):
        total = total + zrecv[v].astype(F32)
    fin[...] = total * factor
    final = remote(fin, rfin, c_send.at[4], c_recv.at[4], sibling)
    final.start()
    b_end(3)
    small = vz[0]
    for v in range(1, 8):
        small = small + vz[v]
    small = small * factor
    for i in range(4):
        o_be[:, 256 * i : 256 * i + 256] = small[i : i + 1]
    for i in range(2):
        cols = slice(256 * i, 256 * i + 256)
        o_br[:, cols] = small[4 + i : 5 + i]
        sg = sigma[:, cols]
        o_gg[:, cols] = small[6 + i : 7 + i] * (sg * (1.0 - sg))

    def place(value, who):
        o_wr[:, pl.ds(pl.multiple_of(256 * who, 256), 256)] = value[0:16]
        for i in range(2):
            o_we[:, pl.ds(pl.multiple_of(512 * who + 256 * i, 256), 256)] = value[16 + 8 * i : 24 + 8 * i]

    place(fin[...], core)
    final.wait_recv()
    place(rfin[...], 1 - core)

    own_out.wait()
    own_gin.wait()
    out_arrive()
    gin_arrive()
    in_sent()
    ct_sent()
    out_sent()
    gin_sent()
    for k in range(4):
        core_copy(k).wait_send()
        for o in range(1, 4):
            first(k, o, True).wait_send()
            second(k, o).wait_send()
    final.wait_send()
    for o in range(1, 8):
        z_copy(o).wait_send()
    for n in range(4):
        for o in B_COUNT[n]:
            b_copy(n, o).wait_send()


def body(inputs, w_expand, b_expand, w_reduce, b_reduce, gate_logit, cotangent):
    rows, width = inputs.shape[1:]
    hidden = w_expand.shape[1]
    block = rows // GROUP
    factor = 1.0 / math.sqrt(lax.axis_size("rep") * lax.axis_size("ctx") * rows)
    any_spec = pl.BlockSpec(memory_space=pl.ANY)
    vmem = pl.BlockSpec(memory_space=pltpu.VMEM)
    dma = pltpu.SemaphoreType.DMA
    results = pl.pallas_call(
        functools.partial(kernel, factor),
        out_shape=(
            jax.ShapeDtypeStruct((GROUP, block, width), BF16),
            jax.ShapeDtypeStruct((GROUP, block, width), BF16),
            jax.ShapeDtypeStruct((8, 1024), F32),
            jax.ShapeDtypeStruct((1, 1024), F32),
            jax.ShapeDtypeStruct((16, 512), F32),
            jax.ShapeDtypeStruct((1, 512), F32),
            jax.ShapeDtypeStruct((1, 512), F32),
        ),
        in_specs=[any_spec, any_spec, vmem, any_spec, vmem, vmem, any_spec],
        out_specs=(any_spec, any_spec, vmem, vmem, vmem, vmem, vmem),
        scratch_shapes=[
            pltpu.VMEM((512, 1024), BF16),
            pltpu.VMEM((1024, 512), BF16),
            pltpu.VMEM((SECTIONS + 1, 16, 16, 256), BF16),
            pltpu.VMEM((SECTIONS + 1, 16, 16, 256), BF16),
            pltpu.VMEM((SECTIONS, 128, 512), F32),
            pltpu.VMEM((SECTIONS, 128, 1), F32),
            pltpu.VMEM((512, 512), BF16),
            pltpu.VMEM((1024, 512), BF16),
            pltpu.VMEM((SECTIONS, 128, 1024), F32),
            pltpu.VMEM((512, 512), BF16),
            pltpu.VMEM((512, 1024), BF16),
            pltpu.VMEM((4, 16, 32, 256), F32),
            pltpu.VMEM((4, 16, 32, 256), BF16),
            pltpu.VMEM((4, 16, 32, 256), BF16),
            pltpu.VMEM((4, 4, 4, 32, 256), BF16),
            pltpu.VMEM((4, 4, 4, 32, 256), BF16),
            pltpu.VMEM((4, 4, 32, 256), BF16),
            pltpu.VMEM((4, 4, 32, 256), BF16),
            pltpu.VMEM((4, 32, 256), BF16),
            pltpu.VMEM((8, 32, 256), BF16),
            pltpu.VMEM((32, 256), F32),
            pltpu.VMEM((32, 256), F32),
            pltpu.VMEM((8, 1024), F32),
            pltpu.VMEM((8, 512), F32),
            pltpu.VMEM((8, 512), F32),
            pltpu.VMEM((8, 256), F32),
            pltpu.VMEM((8, 256), F32),
            pltpu.VMEM((4, 8, 256), F32),
            pltpu.VMEM((4, 8, 256), F32),
            pltpu.VMEM((8, 8, 256), F32),
            dma((6,)),
            dma((4, 16)),
            dma((4, 16)),
            dma((5,)),
            dma((5,)),
            dma((4, 4)),
            dma((4, 4)),
            dma((4, 4)),
            dma((4, 4)),
            dma((8,)),
            dma((8,)),
            dma((4, 8)),
            dma((4, 8)),
        ],
        compiler_params=pltpu.CompilerParams(collective_id=0, has_side_effects=True),
    )(
        inputs.reshape(GROUP, block, width),
        w_expand,
        b_expand.reshape(1, hidden),
        w_reduce,
        b_reduce.reshape(1, 2 * width),
        gate_logit.reshape(1, 2 * width),
        cotangent.reshape(GROUP, block, width),
    )
    out, gin, g_we, g_be, g_wr, g_br, g_gg = results
    return (
        out.reshape(inputs.shape),
        gin.reshape(inputs.shape),
        g_we,
        g_be.reshape(hidden),
        g_wr,
        g_br.reshape(2 * width),
        g_gg.reshape(2 * width),
    )


def solution(mesh):
    return jax.shard_map(
        body,
        mesh=mesh,
        in_specs=(P("rep", "ctx", None), P(), P(), P(), P(), P(), P("rep", "ctx", None)),
        out_specs=(
            P("rep", "ctx", None),
            P("rep", "ctx", None),
            P("ctx", None),
            P(),
            P("ctx", None),
            P(),
            P(),
        ),
        check_vma=False,
    )
```

```python
import functools
import math

import jax
import jax.numpy as jnp
from jax import lax
from jax.experimental import pallas as pl
from jax.experimental.pallas import tpu as pltpu
from jax.sharding import PartitionSpec as P

MESH = pl.DeviceIdType.MESH
F32 = jnp.float32
BF16 = jnp.bfloat16
EPSILON = 1e-05
SECTIONS = 4
GROUP = 16


def dot(a, b, dims):
    return lax.dot_general(a, b, (dims, ((), ())), preferred_element_type=F32)


NN = ((1,), (0,))
NT = ((1,), (1,))


def kernel(
    factor,
    x_ref,
    we_hbm,
    be_hbm,
    wr_hbm,
    br_hbm,
    gl_hbm,
    ct_ref,
    out_ref,
    gin_ref,
    o_we,
    o_be,
    o_wr,
    o_br,
    o_gg,
    we,
    wr,
    be_ref,
    br_ref,
    gl_ref,
    st,
    gst,
    nrm,
    inv,
    norm_t,
    hid_t,
    dgelu,
    gout,
    gpre,
    sib,
    rsib,
    part,
    recv1,
    mid,
    recv2,
    zsend,
    zrecv,
    fin,
    rfin,
    acc_be,
    acc_br,
    acc_gg,
    vec,
    rvec,
    vx,
    vy,
    vz,
    load_sem,
    a_send,
    a_recv,
    c_send,
    c_recv,
    p_send,
    p_recv,
    q_send,
    q_recv,
    z_send,
    z_recv,
    b_send,
    b_recv,
):
    ctx = lax.axis_index("ctx")
    rep = lax.axis_index("rep")
    y = lax.rem(ctx, 4)
    member = lax.div(ctx, 4)
    x = lax.rem(member, 4)
    z_lo = lax.div(member, 4)
    core = lax.rem(rep, 2)
    z_hi = lax.div(rep, 2)
    z = z_hi * 4 + z_lo

    def at_member(m):
        return (m * 4 + y, rep)

    def at_x(v):
        return (z_lo * 16 + v * 4 + y, rep)

    def at_y(v):
        return (member * 4 + v, rep)

    def at_z(v):
        return (lax.rem(v, 4) * 16 + x * 4 + y, lax.div(v, 4) * 2 + core)

    sibling = (ctx, z_hi * 2 + 1 - core)

    def remote(src, dst, send, recv, device):
        return pltpu.make_async_remote_copy(
            src_ref=src, dst_ref=dst, send_sem=send, recv_sem=recv, device_id=device, device_id_type=MESH
        )

    load_we = pltpu.make_async_copy(we_hbm, we, load_sem.at[0])
    load_wr = pltpu.make_async_copy(wr_hbm, wr, load_sem.at[1])
    own_x = pltpu.make_async_copy(x_ref.at[member], st.at[0, member], load_sem.at[2])
    own_ct = pltpu.make_async_copy(ct_ref.at[member], gst.at[SECTIONS, member], load_sem.at[3])
    own_x.start()
    load_we.start()
    load_wr.start()
    own_ct.start()
    small_loads = [
        pltpu.make_async_copy(a, b, load_sem.at[6 + i])
        for i, (a, b) in enumerate(((be_hbm, be_ref), (br_hbm, br_ref), (gl_hbm, gl_ref)))
    ]
    for load in small_loads:
        load.start()

    barrier = pltpu.get_barrier_semaphore()

    def hello(device):
        pl.semaphore_signal(barrier, inc=1, device_id=device, device_id_type=MESH)

    @pl.loop(1, GROUP)
    def _(o):
        hello(at_member(lax.rem(member + o, GROUP)))

    for o in range(1, 4):
        hello(at_y(lax.rem(y + o, 4)))
    for v in range(4):
        hello(at_z((1 - z_hi) * 4 + v))
    hello(sibling)
    pl.semaphore_wait(barrier, 23)

    def exchange(kind, src, dst):
        def copy(o):
            m = lax.rem(member + o, GROUP)
            return remote(src.at[m], dst.at[member], a_send.at[kind, o], a_recv.at[kind, o], at_member(m))

        def start():
            @pl.loop(1, GROUP)
            def _(o):
                copy(o).start()

        def arrive():
            @pl.loop(1, GROUP)
            def _(o):
                m = lax.rem(member + GROUP - o, GROUP)
                remote(src.at[m], dst.at[m], a_send.at[kind, o], a_recv.at[kind, o], at_member(m)).wait_recv()

        def sent():
            @pl.loop(1, GROUP)
            def _(o):
                copy(o).wait_send()

        return start, arrive, sent

    in_start, in_arrive, in_sent = exchange(0, x_ref, st.at[0])
    ct_start, ct_arrive, ct_sent = exchange(1, ct_ref, gst.at[SECTIONS])
    out_start, out_arrive, out_sent = exchange(2, st.at[SECTIONS], out_ref)
    gin_start, gin_arrive, gin_sent = exchange(3, gst.at[0], gin_ref)
    in_start()
    ct_start()

    acc_be[...] = jnp.zeros_like(acc_be)
    acc_br[...] = jnp.zeros_like(acc_br)
    acc_gg[...] = jnp.zeros_like(acc_gg)
    for load in small_loads:
        load.wait()
    sigma = jax.nn.sigmoid(gl_ref[...])

    load_we.wait()
    load_wr.wait()
    own_x.wait()
    in_arrive()

    def joined_of(s):
        lower = st[s, 0:8].reshape(128, 256).astype(F32)
        upper = st[s, 8:16].reshape(128, 256).astype(F32)
        return jnp.concatenate([lower, upper], axis=1)

    def forward(s):
        cols = pl.ds(pl.multiple_of(s * 128, 128), 128)
        joined = joined_of(s)
        centred = joined - jnp.mean(joined, axis=1, keepdims=True)
        inv_std = lax.rsqrt(jnp.mean(centred * centred, axis=1, keepdims=True) + EPSILON)
        normed = centred * inv_std
        nrm[s] = normed
        inv[s] = inv_std
        low = normed.astype(BF16)
        norm_t[:, cols] = low.T
        mixed = sigma * joined + br_ref[...]
        for h in range(4):
            hs = slice(256 * h, 256 * h + 256)
            pre = dot(low, we[:, hs], NN) + be_ref[:, hs]
            cdf = 0.5 + 0.5 * lax.erf(pre * math.sqrt(0.5))
            pdf = jnp.exp(-0.5 * pre * pre) * (1.0 / math.sqrt(2.0 * math.pi))
            dgelu[s, :, hs] = cdf + pre * pdf
            hidden = (pre * cdf).astype(BF16)
            hid_t[hs, cols] = hidden.T
            mixed = mixed + dot(hidden, wr[hs, :], NN)
        result = mixed.astype(BF16)
        for j in range(8):
            st[s + 1, 2 * j] = result[16 * j : 16 * j + 16, :256]
            st[s + 1, 2 * j + 1] = result[16 * j : 16 * j + 16, 256:]

    @pl.loop(0, SECTIONS)
    def _(s):
        forward(s)

    out_start()
    own_out = pltpu.make_async_copy(st.at[SECTIONS, member], out_ref.at[member], load_sem.at[4])
    own_out.start()

    own_ct.wait()
    ct_arrive()

    def rows_of(s):
        return pl.ds(pl.multiple_of(s * 128, 128), 128)

    def upstream(s):
        lower = jnp.concatenate([gst[s + 1, 2 * j] for j in range(8)], axis=0)
        upper = jnp.concatenate([gst[s + 1, 2 * j + 1] for j in range(8)], axis=0)
        gout[rows_of(s), :] = jnp.concatenate([lower, upper], axis=1)

    def fold(v):
        return jnp.sum(v.reshape(16, 8, v.shape[1]), axis=0)

    def backward_hidden(s):
        grad = gout[rows_of(s), :]
        wide = grad.astype(F32)
        acc_br[...] += fold(wide)
        acc_gg[...] += fold(wide * joined_of(s))
        for h in range(4):
            hs = slice(256 * h, 256 * h + 256)
            pre = dot(grad, wr[hs, :], NT) * dgelu[s, :, hs]
            acc_be[:, hs] += fold(pre)
            gpre[rows_of(s), hs] = pre.astype(BF16)

    def backward_joined(s):
        wide = gout[rows_of(s), :].astype(F32)
        gnormed = dot(gpre[rows_of(s), :], we[...], NT)
        normed = nrm[s]
        mean = jnp.mean(gnormed, axis=1, keepdims=True)
        along = jnp.mean(gnormed * normed, axis=1, keepdims=True)
        result = (sigma * wide + inv[s] * (gnormed - mean - normed * along)).astype(BF16)
        gst[s, 0:8] = result[:, :256].reshape(8, 16, 256)
        gst[s, 8:16] = result[:, 256:].reshape(8, 16, 256)

    def core_copy(k):
        return remote(sib.at[k], rsib.at[k], c_send.at[k], c_recv.at[k], sibling)

    def gradient(k, who):
        if k < 2:
            left = hid_t[512 * k : 512 * k + 512, :]
            right = gout[:, pl.ds(pl.multiple_of(256 * who, 256), 256)]
            blocks = dot(left, right, NN).reshape(2, 16, 16, 256)
        else:
            left = norm_t[...]
            right = gpre[:, pl.ds(pl.multiple_of(512 * who + 256 * (k - 2), 256), 256)]
            blocks = dot(left, right, NN).reshape(4, 16, 8, 256)
        return jnp.concatenate([blocks[i] for i in range(blocks.shape[0])], axis=1)

    def give(k):
        sib[k] = gradient(k, 1 - core).astype(BF16)
        core_copy(k).start()

    x_first = (True, False, True, False)

    def first(k, o):
        if x_first[k]:
            v = lax.rem(x + o, 4)
            src = part.at[k, v]
            device = at_x(v)
        else:
            v = lax.rem(y + o, 4)
            src = part.at[k, :, v]
            device = at_y(v)
        return remote(src, recv1.at[k, o], p_send.at[k, o], p_recv.at[k, o], device)

    def second(k, o):
        if x_first[k]:
            v = lax.rem(y + o, 4)
            device = at_y(v)
        else:
            v = lax.rem(x + o, 4)
            device = at_x(v)
        return remote(mid.at[k, v], recv2.at[k, o], q_send.at[k, o], q_recv.at[k, o], device)

    def scatter(k):
        mine = gradient(k, core)
        core_copy(k).wait_recv()
        part[k] = (mine + rsib[k].astype(F32)).astype(BF16).reshape(4, 4, 32, 256)
        for o in range(1, 4):
            first(k, o).start()

    def scatter_again(k):
        for o in range(1, 4):
            first(k, o).wait_recv()
        mine = part[k, x] if x_first[k] else part[k, :, y]
        total = mine.astype(F32)
        for o in range(1, 4):
            total = total + recv1[k, o].astype(F32)
        mid[k] = total.astype(BF16)
        for o in range(1, 4):
            second(k, o).start()

    def reduced(k):
        for o in range(1, 4):
            second(k, o).wait_recv()
        total = (mid[k, y] if x_first[k] else mid[k, x]).astype(F32)
        for o in range(1, 4):
            total = total + recv2[k, o].astype(F32)
        return total

    def z_copy(half, o):
        v = lax.rem(z + o, 8)
        return remote(
            zsend.at[half, lax.rem(v, 4)], zrecv.at[half, z], z_send.at[half, o], z_recv.at[half, o], at_z(v)
        )

    def z_begin(half):
        for o in range(1, 8):
            z_copy(half, o).start()
        zrecv[half, z] = zsend[half, z_lo]

    def final_copy(half):
        return remote(fin.at[half], rfin.at[half], c_send.at[4 + half], c_recv.at[4 + half], sibling)

    def z_end(half):
        for o in range(1, 8):
            v = lax.rem(z + 8 - o, 8)
            remote(
                zsend.at[half, 0], zrecv.at[half, v], z_send.at[half, o], z_recv.at[half, o], at_z(v)
            ).wait_recv()
        total = zrecv[half, 0].astype(F32)
        for v in range(1, 8):
            total = total + zrecv[half, v].astype(F32)
        fin[half] = total * factor
        final_copy(half).start()

    def b_copy(n, o):
        sems = (b_send.at[n, o], b_recv.at[n, o])
        if n == 0:
            return remote(vec, rvec, *sems, sibling)
        if n == 1:
            return remote(vx.at[x], vx.at[x], *sems, at_x(lax.rem(x + o, 4)))
        if n == 2:
            return remote(vy.at[y], vy.at[y], *sems, at_y(lax.rem(y + o, 4)))
        return remote(vz.at[z], vz.at[z], *sems, at_z(lax.rem(z + o, 8)))

    def b_arrive(n, o):
        sems = (b_send.at[n, o], b_recv.at[n, o])
        if n == 0:
            remote(vec, rvec, *sems, sibling).wait_recv()
        elif n == 1:
            v = lax.rem(x + 4 - o, 4)
            remote(vx.at[v], vx.at[v], *sems, at_x(v)).wait_recv()
        elif n == 2:
            v = lax.rem(y + 4 - o, 4)
            remote(vy.at[v], vy.at[v], *sems, at_y(v)).wait_recv()
        else:
            v = lax.rem(z + 8 - o, 8)
            remote(vz.at[v], vz.at[v], *sems, at_z(v)).wait_recv()

    B_COUNT = (range(0, 1), range(1, 4), range(1, 4), range(1, 8))

    def b_begin(n):
        for o in B_COUNT[n]:
            b_copy(n, o).start()

    def b_end(n):
        for o in B_COUNT[n]:
            b_arrive(n, o)

    @pl.loop(0, SECTIONS - 1)
    def _(i):
        s = SECTIONS - 1 - i
        upstream(s)
        backward_hidden(s)
        backward_joined(s)

    def put(row, v):
        total = jnp.sum(v, axis=0, keepdims=True)
        for i in range(v.shape[1] // 256):
            vec[row + i : row + i + 1, :] = total[:, 256 * i : 256 * i + 256]

    upstream(0)
    give(0)
    give(1)
    backward_hidden(0)
    scatter(0)
    scatter(1)
    give(2)
    give(3)
    backward_joined(0)
    put(0, acc_be[...])
    put(4, acc_br[...])
    put(6, acc_gg[...])
    scatter(2)
    scatter(3)
    b_begin(0)
    gin_start()
    own_gin = pltpu.make_async_copy(gst.at[0, member], gin_ref.at[member], load_sem.at[5])
    own_gin.start()
    scatter_again(0)
    scatter_again(1)
    b_end(0)
    vx[x] = vec[...] + rvec[...]
    b_begin(1)
    for k in range(2):
        block = reduced(k)
        for i in range(2):
            zsend[0, 2 * k + i] = block[16 * i : 16 * i + 16].astype(BF16)
    z_begin(0)
    scatter_again(2)
    scatter_again(3)
    b_end(1)
    vy[y] = (vx[0] + vx[1]) + (vx[2] + vx[3])
    b_begin(2)
    left = reduced(2)
    right = reduced(3)
    for i in range(4):
        rows = slice(8 * i, 8 * i + 8)
        zsend[1, i] = jnp.concatenate([left[rows], right[rows]], axis=0).astype(BF16)
    z_begin(1)
    b_end(2)
    vz[z] = (vy[0] + vy[1]) + (vy[2] + vy[3])
    b_begin(3)
    z_end(0)
    z_end(1)
    b_end(3)
    small = vz[0]
    for v in range(1, 8):
        small = small + vz[v]
    small = small * factor
    for i in range(4):
        o_be[:, 256 * i : 256 * i + 256] = small[i : i + 1]
    for i in range(2):
        cols = slice(256 * i, 256 * i + 256)
        o_br[:, cols] = small[4 + i : 5 + i]
        sg = sigma[:, cols]
        o_gg[:, cols] = small[6 + i : 7 + i] * (sg * (1.0 - sg))

    def place(half, value, who):
        if half == 0:
            o_wr[:, pl.ds(pl.multiple_of(256 * who, 256), 256)] = value
        else:
            for i in range(2):
                o_we[:, pl.ds(pl.multiple_of(512 * who + 256 * i, 256), 256)] = value[8 * i : 8 * i + 8]

    for half in range(2):
        place(half, fin[half], core)
    for half in range(2):
        final_copy(half).wait_recv()
        place(half, rfin[half], 1 - core)

    own_out.wait()
    own_gin.wait()
    out_arrive()
    gin_arrive()
    in_sent()
    ct_sent()
    out_sent()
    gin_sent()
    for k in range(4):
        core_copy(k).wait_send()
        for o in range(1, 4):
            first(k, o).wait_send()
            second(k, o).wait_send()
    for half in range(2):
        final_copy(half).wait_send()
        for o in range(1, 8):
            z_copy(half, o).wait_send()
    for n in range(4):
        for o in B_COUNT[n]:
            b_copy(n, o).wait_send()


def finish(*refs):
    n = len(refs) // 2
    copies = [pltpu.make_async_copy(refs[i], refs[n + i], refs[2 * n].at[i]) for i in range(n)]
    for copy in copies:
        copy.start()
    for copy in copies:
        copy.wait()


def hand_on(arrays):
    n = len(arrays)
    return pl.pallas_call(
        finish,
        out_shape=tuple(jax.ShapeDtypeStruct(a.shape, a.dtype) for a in arrays),
        in_specs=[pl.BlockSpec(memory_space=pl.ANY)] * n,
        out_specs=(pl.BlockSpec(memory_space=pltpu.HBM),) * n,
        scratch_shapes=[pltpu.SemaphoreType.DMA((n,))],
        compiler_params=pltpu.CompilerParams(vmem_limit_bytes=1024 * 1024),
    )(*arrays)


def body(inputs, w_expand, b_expand, w_reduce, b_reduce, gate_logit, cotangent):
    rows, width = inputs.shape[1:]
    hidden = w_expand.shape[1]
    block = rows // GROUP
    factor = 1.0 / math.sqrt(lax.axis_size("rep") * lax.axis_size("ctx") * rows)
    any_spec = pl.BlockSpec(memory_space=pl.ANY)
    vmem = pl.BlockSpec(memory_space=pltpu.VMEM)
    dma = pltpu.SemaphoreType.DMA
    results = pl.pallas_call(
        functools.partial(kernel, factor),
        out_shape=(
            jax.ShapeDtypeStruct((GROUP, block, width), BF16),
            jax.ShapeDtypeStruct((GROUP, block, width), BF16),
            jax.ShapeDtypeStruct((8, 1024), F32),
            jax.ShapeDtypeStruct((1, 1024), F32),
            jax.ShapeDtypeStruct((16, 512), F32),
            jax.ShapeDtypeStruct((1, 512), F32),
            jax.ShapeDtypeStruct((1, 512), F32),
        ),
        in_specs=[pl.BlockSpec(memory_space=pltpu.HBM)] * 7,
        out_specs=(any_spec, any_spec, vmem, vmem, vmem, vmem, vmem),
        scratch_shapes=[
            pltpu.VMEM((512, 1024), BF16),
            pltpu.VMEM((1024, 512), BF16),
            pltpu.VMEM((1, 1024), F32),
            pltpu.VMEM((1, 512), F32),
            pltpu.VMEM((1, 512), F32),
            pltpu.VMEM((SECTIONS + 1, 16, 16, 256), BF16),
            pltpu.VMEM((SECTIONS + 1, 16, 16, 256), BF16),
            pltpu.VMEM((SECTIONS, 128, 512), F32),
            pltpu.VMEM((SECTIONS, 128, 1), F32),
            pltpu.VMEM((512, 512), BF16),
            pltpu.VMEM((1024, 512), BF16),
            pltpu.VMEM((SECTIONS, 128, 1024), F32),
            pltpu.VMEM((512, 512), BF16),
            pltpu.VMEM((512, 1024), BF16),
            pltpu.VMEM((4, 16, 32, 256), BF16),
            pltpu.VMEM((4, 16, 32, 256), BF16),
            pltpu.VMEM((4, 4, 4, 32, 256), BF16),
            pltpu.VMEM((4, 4, 4, 32, 256), BF16),
            pltpu.VMEM((4, 4, 32, 256), BF16),
            pltpu.VMEM((4, 4, 32, 256), BF16),
            pltpu.VMEM((2, 4, 16, 256), BF16),
            pltpu.VMEM((2, 8, 16, 256), BF16),
            pltpu.VMEM((2, 16, 256), F32),
            pltpu.VMEM((2, 16, 256), F32),
            pltpu.VMEM((8, 1024), F32),
            pltpu.VMEM((8, 512), F32),
            pltpu.VMEM((8, 512), F32),
            pltpu.VMEM((8, 256), F32),
            pltpu.VMEM((8, 256), F32),
            pltpu.VMEM((4, 8, 256), F32),
            pltpu.VMEM((4, 8, 256), F32),
            pltpu.VMEM((8, 8, 256), F32),
            dma((9,)),
            dma((4, 16)),
            dma((4, 16)),
            dma((6,)),
            dma((6,)),
            dma((4, 4)),
            dma((4, 4)),
            dma((4, 4)),
            dma((4, 4)),
            dma((2, 8)),
            dma((2, 8)),
            dma((4, 8)),
            dma((4, 8)),
        ],
        compiler_params=pltpu.CompilerParams(collective_id=0, has_side_effects=True, vmem_limit_bytes=24 * 1024 * 1024),
    )(
        *(
            pltpu.with_memory_space_constraint(value, pltpu.HBM)
            for value in (
                inputs.reshape(GROUP, block, width),
                w_expand,
                b_expand.reshape(1, hidden),
                w_reduce,
                b_reduce.reshape(1, 2 * width),
                gate_logit.reshape(1, 2 * width),
                cotangent.reshape(GROUP, block, width),
            )
        )
    )
    out, gin, g_we, g_be, g_wr, g_br, g_gg = hand_on(results)
    return (
        out.reshape(inputs.shape),
        gin.reshape(inputs.shape),
        g_we,
        g_be.reshape(hidden),
        g_wr,
        g_br.reshape(2 * width),
        g_gg.reshape(2 * width),
    )


def solution(mesh):
    return jax.shard_map(
        body,
        mesh=mesh,
        in_specs=(P("rep", "ctx", None), P(), P(), P(), P(), P(), P("rep", "ctx", None)),
        out_specs=(
            P("rep", "ctx", None),
            P("rep", "ctx", None),
            P("ctx", None),
            P(),
            P("ctx", None),
            P(),
            P(),
        ),
        check_vma=False,
    )
```

```python
import functools
import math

import jax
import jax.numpy as jnp
from jax import lax
from jax.experimental import pallas as pl
from jax.experimental.pallas import tpu as pltpu
from jax.sharding import PartitionSpec as P

MESH = pl.DeviceIdType.MESH
F32 = jnp.float32
BF16 = jnp.bfloat16
EPSILON = 1e-05
SECTIONS = 4
GROUP = 16


def dot(a, b, dims):
    return lax.dot_general(a, b, (dims, ((), ())), preferred_element_type=F32)


NN = ((1,), (0,))
NT = ((1,), (1,))


def kernel(
    factor,
    x_ref,
    we_hbm,
    be_hbm,
    wr_hbm,
    br_hbm,
    gl_hbm,
    ct_ref,
    out_ref,
    gin_ref,
    o_we,
    o_be,
    o_wr,
    o_br,
    o_gg,
    we,
    wr,
    be_ref,
    br_ref,
    gl_ref,
    st,
    gst,
    nrm,
    inv,
    norm_t,
    hid_t,
    dgelu,
    gout,
    gpre,
    sib,
    rsib,
    part,
    recv1,
    mid,
    recv2,
    fin,
    rfin,
    acc_be,
    acc_br,
    acc_gg,
    vec,
    rvec,
    vx,
    vy,
    vz,
    small,
    load_sem,
    a_send,
    a_recv,
    c_send,
    c_recv,
    p_send,
    p_recv,
    q_send,
    q_recv,
    f_send,
    f_recv,
    b_send,
    b_recv,
):
    ctx = lax.axis_index("ctx")
    rep = lax.axis_index("rep")
    y = lax.rem(ctx, 4)
    member = lax.div(ctx, 4)
    x = lax.rem(member, 4)
    z_lo = lax.div(member, 4)
    core = lax.rem(rep, 2)
    z_hi = lax.div(rep, 2)
    z = z_hi * 4 + z_lo

    def at_member(m):
        return (m * 4 + y, rep)

    def at(px, py, pz, pc):
        return (lax.rem(pz, 4) * 16 + px * 4 + py, lax.div(pz, 4) * 2 + pc)

    def at_x(v):
        return at(v, y, z, core)

    def at_y(v):
        return at(x, v, z, core)

    def at_z(v):
        return at(x, y, v, core)

    sibling = (ctx, z_hi * 2 + 1 - core)
    across = (ctx, (1 - z_hi) * 2 + core)
    opposite = (ctx, (1 - z_hi) * 2 + 1 - core)

    def remote(src, dst, send, recv, device):
        return pltpu.make_async_remote_copy(
            src_ref=src, dst_ref=dst, send_sem=send, recv_sem=recv, device_id=device, device_id_type=MESH
        )

    load_we = pltpu.make_async_copy(we_hbm, we, load_sem.at[0])
    load_wr = pltpu.make_async_copy(wr_hbm, wr, load_sem.at[1])
    own_x = pltpu.make_async_copy(x_ref.at[member], st.at[0, member], load_sem.at[2])
    own_ct = pltpu.make_async_copy(ct_ref.at[member], gst.at[SECTIONS, member], load_sem.at[3])
    own_x.start()
    load_we.start()
    load_wr.start()
    own_ct.start()
    small_loads = [
        pltpu.make_async_copy(a, b, load_sem.at[6 + i])
        for i, (a, b) in enumerate(((be_hbm, be_ref), (br_hbm, br_ref), (gl_hbm, gl_ref)))
    ]
    for load in small_loads:
        load.start()

    barrier = pltpu.get_barrier_semaphore()

    def hello(device):
        pl.semaphore_signal(barrier, inc=1, device_id=device, device_id_type=MESH)

    @pl.loop(1, 32)
    def _(o):
        v = lax.rem(z + lax.rem(o, 8), 8)
        hello(at(lax.rem(x + lax.div(o, 8), 4), y, v, core))

    @pl.loop(0, 15)
    def _(o):
        v = lax.rem(z + 6 + lax.rem(o, 5), 8)
        hello(at(x, lax.rem(y + 1 + lax.div(o, 5), 4), v, core))

    hello(sibling)
    hello(opposite)
    pl.semaphore_wait(barrier, 48)

    def exchange(kind, src, dst):
        def copy(o):
            m = lax.rem(member + o, GROUP)
            return remote(src.at[m], dst.at[member], a_send.at[kind, o], a_recv.at[kind, o], at_member(m))

        def start():
            @pl.loop(1, GROUP)
            def _(o):
                copy(o).start()

        def arrive():
            @pl.loop(1, GROUP)
            def _(o):
                m = lax.rem(member + GROUP - o, GROUP)
                remote(src.at[m], dst.at[m], a_send.at[kind, o], a_recv.at[kind, o], at_member(m)).wait_recv()

        def sent():
            @pl.loop(1, GROUP)
            def _(o):
                copy(o).wait_send()

        return start, arrive, sent

    in_start, in_arrive, in_sent = exchange(0, x_ref, st.at[0])
    ct_start, ct_arrive, ct_sent = exchange(1, ct_ref, gst.at[SECTIONS])
    out_start, out_arrive, out_sent = exchange(2, st.at[SECTIONS], out_ref)
    gin_start, gin_arrive, gin_sent = exchange(3, gst.at[0], gin_ref)
    in_start()
    ct_start()

    acc_be[...] = jnp.zeros_like(acc_be)
    acc_br[...] = jnp.zeros_like(acc_br)
    acc_gg[...] = jnp.zeros_like(acc_gg)
    for load in small_loads:
        load.wait()
    sigma = jax.nn.sigmoid(gl_ref[...])

    load_we.wait()
    load_wr.wait()
    own_x.wait()
    in_arrive()

    def joined_of(s):
        lower = st[s, 0:8].reshape(128, 256).astype(F32)
        upper = st[s, 8:16].reshape(128, 256).astype(F32)
        return jnp.concatenate([lower, upper], axis=1)

    def forward(s):
        cols = pl.ds(pl.multiple_of(s * 128, 128), 128)
        joined = joined_of(s)
        centred = joined - jnp.mean(joined, axis=1, keepdims=True)
        inv_std = lax.rsqrt(jnp.mean(centred * centred, axis=1, keepdims=True) + EPSILON)
        normed = centred * inv_std
        nrm[s] = normed
        inv[s] = inv_std
        low = normed.astype(BF16)
        norm_t[:, cols] = low.T
        mixed = sigma * joined + br_ref[...]
        for h in range(4):
            hs = slice(256 * h, 256 * h + 256)
            pre = dot(low, we[:, hs], NN) + be_ref[:, hs]
            cdf = 0.5 + 0.5 * lax.erf(pre * math.sqrt(0.5))
            pdf = jnp.exp(-0.5 * pre * pre) * (1.0 / math.sqrt(2.0 * math.pi))
            dgelu[s, :, hs] = cdf + pre * pdf
            hidden = (pre * cdf).astype(BF16)
            hid_t[hs, cols] = hidden.T
            mixed = mixed + dot(hidden, wr[hs, :], NN)
        result = mixed.astype(BF16)
        for j in range(8):
            st[s + 1, 2 * j] = result[16 * j : 16 * j + 16, :256]
            st[s + 1, 2 * j + 1] = result[16 * j : 16 * j + 16, 256:]

    @pl.loop(0, SECTIONS)
    def _(s):
        forward(s)

    out_start()
    own_out = pltpu.make_async_copy(st.at[SECTIONS, member], out_ref.at[member], load_sem.at[4])
    own_out.start()

    own_ct.wait()
    ct_arrive()

    def rows_of(s):
        return pl.ds(pl.multiple_of(s * 128, 128), 128)

    def upstream(s):
        lower = jnp.concatenate([gst[s + 1, 2 * j] for j in range(8)], axis=0)
        upper = jnp.concatenate([gst[s + 1, 2 * j + 1] for j in range(8)], axis=0)
        gout[rows_of(s), :] = jnp.concatenate([lower, upper], axis=1)

    def fold(v):
        return jnp.sum(v.reshape(16, 8, v.shape[1]), axis=0)

    def backward_hidden(s):
        grad = gout[rows_of(s), :]
        wide = grad.astype(F32)
        acc_br[...] += fold(wide)
        acc_gg[...] += fold(wide * joined_of(s))
        for h in range(4):
            hs = slice(256 * h, 256 * h + 256)
            pre = dot(grad, wr[hs, :], NT) * dgelu[s, :, hs]
            acc_be[:, hs] += fold(pre)
            gpre[rows_of(s), hs] = pre.astype(BF16)

    def backward_joined(s):
        wide = gout[rows_of(s), :].astype(F32)
        gnormed = dot(gpre[rows_of(s), :], we[...], NT)
        normed = nrm[s]
        mean = jnp.mean(gnormed, axis=1, keepdims=True)
        along = jnp.mean(gnormed * normed, axis=1, keepdims=True)
        result = (sigma * wide + inv[s] * (gnormed - mean - normed * along)).astype(BF16)
        gst[s, 0:8] = result[:, :256].reshape(8, 16, 256)
        gst[s, 8:16] = result[:, 256:].reshape(8, 16, 256)

    def core_copy(k):
        return remote(sib.at[k], rsib.at[k], c_send.at[k], c_recv.at[k], sibling)

    def reduce_quarters(who):
        right = gout[:, pl.ds(pl.multiple_of(256 * who, 256), 256)]
        blocks = dot(hid_t[...], right, NN).reshape(4, 16, 16, 256)
        return [[blocks[q, :, :, 128 * k : 128 * k + 128] for q in range(4)] for k in range(2)]

    def expand_quarters(k, who):
        right = gpre[:, pl.ds(pl.multiple_of(512 * who + 256 * (k - 2), 256), 256)]
        blocks = dot(norm_t[...], right, NN).reshape(4, 16, 8, 256)
        return [jnp.concatenate([blocks[q, :, :, :128], blocks[q, :, :, 128:]], axis=1) for q in range(4)]

    def give(k, quarters):
        for q in range(4):
            sib[k, :, q] = quarters[q].astype(BF16)
        core_copy(k).start()

    x_first = (True, False, True, False)

    def first(k, o):
        if x_first[k]:
            v = lax.rem(x + o, 4)
            src = part.at[k, v]
            device = at_x(v)
        else:
            v = lax.rem(y + o, 4)
            src = part.at[k, :, v]
            device = at_y(v)
        return remote(src, recv1.at[k, o], p_send.at[k, o], p_recv.at[k, o], device)

    def scatter(k, quarters):
        core_copy(k).wait_recv()
        for q in range(4):
            total = quarters[q] + rsib[k, :, q].astype(F32)
            part[k, :, :, q] = total.astype(BF16).reshape(4, 4, 16, 128)
        for o in range(1, 4):
            first(k, o).start()

    def second(k, j):
        dv, step = divmod(j, 4)
        dz = (0, 1, 2 if x_first[k] else 6, 7)[step]
        v = lax.rem((y if x_first[k] else x) + dv, 4)
        pz = lax.rem(z + dz, 8)
        device = at(x, v, pz, core) if x_first[k] else at(v, y, pz, core)
        return remote(
            mid.at[k, v, lax.rem(pz, 4)], recv2.at[k, j], q_send.at[k, j], q_recv.at[k, j], device
        )

    def scatter_again(k):
        for o in range(1, 4):
            first(k, o).wait_recv()
        total = (part[k, x] if x_first[k] else part[k, :, y]).astype(F32)
        for o in range(1, 4):
            total = total + recv1[k, o].astype(F32)
        mid[k] = total.astype(BF16)
        for j in range(1, 16):
            second(k, j).start()

    def final_copy(half, n):
        device = (sibling, across, opposite)[n]
        return remote(fin.at[half], rfin.at[n, half], f_send.at[half, n], f_recv.at[half, n], device)

    def reduced(half):
        for k in (2 * half, 2 * half + 1):
            for j in range(1, 16):
                second(k, j).wait_recv()
            total = mid[k, y if x_first[k] else x, z_lo].astype(F32)
            for j in range(1, 16):
                total = total + recv2[k, j].astype(F32)
            fin[half, k - 2 * half] = total.astype(BF16)
        for n in range(3):
            final_copy(half, n).start()

    def b_copy(n, o):
        sems = (b_send.at[n, o], b_recv.at[n, o])
        if n == 0:
            return remote(vec.at[1 - core], rvec, *sems, sibling)
        if n == 1:
            return remote(vx.at[x], vx.at[x], *sems, at_x(lax.rem(x + o, 4)))
        if n == 2:
            return remote(vy.at[y], vy.at[y], *sems, at_y(lax.rem(y + o, 4)))
        if n == 3:
            return remote(vz.at[z], vz.at[z], *sems, at_z(lax.rem(z + o, 8)))
        return remote(small.at[core], small.at[core], *sems, sibling)

    def b_arrive(n, o):
        sems = (b_send.at[n, o], b_recv.at[n, o])
        if n == 0:
            remote(vec.at[core], rvec, *sems, sibling).wait_recv()
        elif n == 1:
            v = lax.rem(x + 4 - o, 4)
            remote(vx.at[v], vx.at[v], *sems, at_x(v)).wait_recv()
        elif n == 2:
            v = lax.rem(y + 4 - o, 4)
            remote(vy.at[v], vy.at[v], *sems, at_y(v)).wait_recv()
        elif n == 3:
            v = lax.rem(z + 8 - o, 8)
            remote(vz.at[v], vz.at[v], *sems, at_z(v)).wait_recv()
        else:
            remote(small.at[1 - core], small.at[1 - core], *sems, sibling).wait_recv()

    B_COUNT = (range(0, 1), range(1, 4), range(1, 4), range(1, 8), range(0, 1))

    def b_begin(n):
        for o in B_COUNT[n]:
            b_copy(n, o).start()

    def b_end(n):
        for o in B_COUNT[n]:
            b_arrive(n, o)

    @pl.loop(0, SECTIONS - 1)
    def _(i):
        s = SECTIONS - 1 - i
        upstream(s)
        backward_hidden(s)
        backward_joined(s)

    def put(half, row, v):
        total = jnp.sum(v, axis=0, keepdims=True)
        for i in range(v.shape[1] // 128):
            vec[half, row + i : row + i + 1, :] = total[:, 128 * i : 128 * i + 128]

    upstream(0)
    for k, quarters in enumerate(reduce_quarters(1 - core)):
        give(k, quarters)
    backward_hidden(0)
    for k, quarters in enumerate(reduce_quarters(core)):
        scatter(k, quarters)
    for k in (2, 3):
        give(k, expand_quarters(k, 1 - core))
    backward_joined(0)
    put(0, 0, acc_be[...])
    put(1, 0, acc_br[...])
    put(1, 4, acc_gg[...])
    b_begin(0)
    for k in (2, 3):
        scatter(k, expand_quarters(k, core))
    b_end(0)
    vx[x] = vec[core] + rvec[...]
    b_begin(1)
    gin_start()
    own_gin = pltpu.make_async_copy(gst.at[0, member], gin_ref.at[member], load_sem.at[5])
    own_gin.start()
    scatter_again(0)
    scatter_again(1)
    b_end(1)
    vy[y] = (vx[0] + vx[1]) + (vx[2] + vx[3])
    b_begin(2)
    scatter_again(2)
    scatter_again(3)
    b_end(2)
    vz[z] = (vy[0] + vy[1]) + (vy[2] + vy[3])
    b_begin(3)
    reduced(0)
    reduced(1)
    b_end(3)
    total = vz[0]
    for v in range(1, 8):
        total = total + vz[v]
    small[core] = total * factor
    b_begin(4)

    def place(half, value, who):
        for k in range(2):
            if half == 0:
                o_wr[:, pl.ds(pl.multiple_of(256 * who + 128 * k, 128), 128)] = value[k]
            else:
                for i in range(2):
                    cols = pl.ds(pl.multiple_of(512 * who + 256 * k + 128 * i, 128), 128)
                    o_we[:, cols] = value[k, 8 * i : 8 * i + 8]

    for half in range(2):
        for n in range(3):
            final_copy(half, n).wait_recv()
        place(half, (fin[half].astype(F32) + rfin[1, half].astype(F32)) * factor, core)
        place(half, (rfin[0, half].astype(F32) + rfin[2, half].astype(F32)) * factor, 1 - core)
    b_end(4)
    for i in range(8):
        o_be[:, 128 * i : 128 * i + 128] = small[0, i : i + 1]
    for i in range(4):
        cols = slice(128 * i, 128 * i + 128)
        o_br[:, cols] = small[1, i : i + 1]
        sg = sigma[:, cols]
        o_gg[:, cols] = small[1, 4 + i : 5 + i] * (sg * (1.0 - sg))

    own_out.wait()
    own_gin.wait()
    out_arrive()
    gin_arrive()
    in_sent()
    ct_sent()
    out_sent()
    gin_sent()
    for k in range(4):
        core_copy(k).wait_send()
        for o in range(1, 4):
            first(k, o).wait_send()
        for j in range(1, 16):
            second(k, j).wait_send()
    for half in range(2):
        for n in range(3):
            final_copy(half, n).wait_send()
    for n in range(5):
        for o in B_COUNT[n]:
            b_copy(n, o).wait_send()


def finish(*refs):
    n = len(refs) // 2
    copies = [pltpu.make_async_copy(refs[i], refs[n + i], refs[2 * n].at[i]) for i in range(n)]
    for copy in copies:
        copy.start()
    for copy in copies:
        copy.wait()


def hand_on(arrays):
    n = len(arrays)
    return pl.pallas_call(
        finish,
        out_shape=tuple(jax.ShapeDtypeStruct(a.shape, a.dtype) for a in arrays),
        in_specs=[pl.BlockSpec(memory_space=pl.ANY)] * n,
        out_specs=(pl.BlockSpec(memory_space=pltpu.HBM),) * n,
        scratch_shapes=[pltpu.SemaphoreType.DMA((n,))],
        compiler_params=pltpu.CompilerParams(vmem_limit_bytes=1024 * 1024),
    )(*arrays)


def body(inputs, w_expand, b_expand, w_reduce, b_reduce, gate_logit, cotangent):
    rows, width = inputs.shape[1:]
    hidden = w_expand.shape[1]
    block = rows // GROUP
    factor = 1.0 / math.sqrt(lax.axis_size("rep") * lax.axis_size("ctx") * rows)
    any_spec = pl.BlockSpec(memory_space=pl.ANY)
    vmem = pl.BlockSpec(memory_space=pltpu.VMEM)
    dma = pltpu.SemaphoreType.DMA
    results = pl.pallas_call(
        functools.partial(kernel, factor),
        out_shape=(
            jax.ShapeDtypeStruct((GROUP, block, width), BF16),
            jax.ShapeDtypeStruct((GROUP, block, width), BF16),
            jax.ShapeDtypeStruct((8, 1024), F32),
            jax.ShapeDtypeStruct((1, 1024), F32),
            jax.ShapeDtypeStruct((16, 512), F32),
            jax.ShapeDtypeStruct((1, 512), F32),
            jax.ShapeDtypeStruct((1, 512), F32),
        ),
        in_specs=[pl.BlockSpec(memory_space=pltpu.HBM)] * 7,
        out_specs=(any_spec, any_spec, vmem, vmem, vmem, vmem, vmem),
        scratch_shapes=[
            pltpu.VMEM((512, 1024), BF16),
            pltpu.VMEM((1024, 512), BF16),
            pltpu.VMEM((1, 1024), F32),
            pltpu.VMEM((1, 512), F32),
            pltpu.VMEM((1, 512), F32),
            pltpu.VMEM((SECTIONS + 1, 16, 16, 256), BF16),
            pltpu.VMEM((SECTIONS + 1, 16, 16, 256), BF16),
            pltpu.VMEM((SECTIONS, 128, 512), F32),
            pltpu.VMEM((SECTIONS, 128, 1), F32),
            pltpu.VMEM((512, 512), BF16),
            pltpu.VMEM((1024, 512), BF16),
            pltpu.VMEM((SECTIONS, 128, 1024), F32),
            pltpu.VMEM((512, 512), BF16),
            pltpu.VMEM((512, 1024), BF16),
            pltpu.VMEM((4, 16, 4, 16, 128), BF16),
            pltpu.VMEM((4, 16, 4, 16, 128), BF16),
            pltpu.VMEM((4, 4, 4, 4, 16, 128), BF16),
            pltpu.VMEM((4, 4, 4, 4, 16, 128), BF16),
            pltpu.VMEM((4, 4, 4, 16, 128), BF16),
            pltpu.VMEM((4, 16, 16, 128), BF16),
            pltpu.VMEM((2, 2, 16, 128), BF16),
            pltpu.VMEM((3, 2, 2, 16, 128), BF16),
            pltpu.VMEM((8, 1024), F32),
            pltpu.VMEM((8, 512), F32),
            pltpu.VMEM((8, 512), F32),
            pltpu.VMEM((2, 8, 128), F32),
            pltpu.VMEM((8, 128), F32),
            pltpu.VMEM((4, 8, 128), F32),
            pltpu.VMEM((4, 8, 128), F32),
            pltpu.VMEM((8, 8, 128), F32),
            pltpu.VMEM((2, 8, 128), F32),
            dma((9,)),
            dma((4, 16)),
            dma((4, 16)),
            dma((4,)),
            dma((4,)),
            dma((4, 4)),
            dma((4, 4)),
            dma((4, 16)),
            dma((4, 16)),
            dma((2, 3)),
            dma((2, 3)),
            dma((5, 8)),
            dma((5, 8)),
        ],
        compiler_params=pltpu.CompilerParams(collective_id=0, has_side_effects=True, vmem_limit_bytes=24 * 1024 * 1024),
    )(
        *(
            pltpu.with_memory_space_constraint(value, pltpu.HBM)
            for value in (
                inputs.reshape(GROUP, block, width),
                w_expand,
                b_expand.reshape(1, hidden),
                w_reduce,
                b_reduce.reshape(1, 2 * width),
                gate_logit.reshape(1, 2 * width),
                cotangent.reshape(GROUP, block, width),
            )
        )
    )
    out, gin, g_we, g_be, g_wr, g_br, g_gg = hand_on(results)
    return (
        out.reshape(inputs.shape),
        gin.reshape(inputs.shape),
        g_we,
        g_be.reshape(hidden),
        g_wr,
        g_br.reshape(2 * width),
        g_gg.reshape(2 * width),
    )


def solution(mesh):
    return jax.shard_map(
        body,
        mesh=mesh,
        in_specs=(P("rep", "ctx", None), P(), P(), P(), P(), P(), P("rep", "ctx", None)),
        out_specs=(
            P("rep", "ctx", None),
            P("rep", "ctx", None),
            P("ctx", None),
            P(),
            P("ctx", None),
            P(),
            P(),
        ),
        check_vma=False,
    )
```

```python
import functools
import math

import jax
import jax.numpy as jnp
from jax import lax
from jax.experimental import pallas as pl
from jax.experimental.pallas import tpu as pltpu
from jax.sharding import PartitionSpec as P

MESH = pl.DeviceIdType.MESH
F32 = jnp.float32
BF16 = jnp.bfloat16
EPSILON = 1e-05
SECTIONS = 4
GROUP = 16


def dot(a, b, dims):
    return lax.dot_general(a, b, (dims, ((), ())), preferred_element_type=F32)


NN = ((1,), (0,))
NT = ((1,), (1,))


def kernel(
    factor,
    x_ref,
    we_hbm,
    be_hbm,
    wr_hbm,
    br_hbm,
    gl_hbm,
    ct_ref,
    out_ref,
    gin_ref,
    o_we,
    o_be,
    o_wr,
    o_br,
    o_gg,
    we,
    wr,
    be_ref,
    br_ref,
    gl_ref,
    st,
    gst,
    nrm,
    inv,
    norm_t,
    hid_t,
    dgelu,
    gout,
    gpre,
    hid_s,
    norm_s,
    gout_s,
    gpre_s,
    own,
    part,
    recv1,
    mid,
    recv2,
    zsend,
    zrecv,
    fin,
    rfin,
    acc_be,
    acc_br,
    acc_gg,
    vec,
    rvec,
    vx,
    vy,
    vz,
    small,
    load_sem,
    a_send,
    a_recv,
    c_send,
    c_recv,
    s_send,
    s_recv,
    p_send,
    p_recv,
    q_send,
    q_recv,
    z_send,
    z_recv,
    b_send,
    b_recv,
):
    ctx = lax.axis_index("ctx")
    rep = lax.axis_index("rep")
    y = lax.rem(ctx, 4)
    member = lax.div(ctx, 4)
    x = lax.rem(member, 4)
    z_lo = lax.div(member, 4)
    core = lax.rem(rep, 2)
    z_hi = lax.div(rep, 2)
    z = z_hi * 4 + z_lo

    def at_member(m):
        return (m * 4 + y, rep)

    def at_x(v):
        return (z_lo * 16 + v * 4 + y, rep)

    def at_y(v):
        return (member * 4 + v, rep)

    def at_z(v):
        return (lax.rem(v, 4) * 16 + x * 4 + y, lax.div(v, 4) * 2 + core)

    sibling = (ctx, z_hi * 2 + 1 - core)

    def remote(src, dst, send, recv, device):
        return pltpu.make_async_remote_copy(
            src_ref=src, dst_ref=dst, send_sem=send, recv_sem=recv, device_id=device, device_id_type=MESH
        )

    barrier = pltpu.get_barrier_semaphore()

    def hello(device):
        pl.semaphore_signal(barrier, inc=1, device_id=device, device_id_type=MESH)

    @pl.loop(1, GROUP)
    def _(o):
        hello(at_member(lax.rem(member + o, GROUP)))

    for o in range(1, 4):
        hello(at_y(lax.rem(y + o, 4)))
    for v in range(4):
        hello(at_z((1 - z_hi) * 4 + v))
    hello(sibling)
    load_we = pltpu.make_async_copy(we_hbm, we, load_sem.at[0])
    load_wr = pltpu.make_async_copy(wr_hbm, wr, load_sem.at[1])
    own_x = pltpu.make_async_copy(x_ref.at[member], st.at[0, member], load_sem.at[2])
    own_ct = pltpu.make_async_copy(ct_ref.at[member], gst.at[SECTIONS, member], load_sem.at[3])
    own_x.start()
    load_we.start()
    load_wr.start()
    own_ct.start()
    small_loads = [
        pltpu.make_async_copy(a, b, load_sem.at[6 + i])
        for i, (a, b) in enumerate(((be_hbm, be_ref), (br_hbm, br_ref), (gl_hbm, gl_ref)))
    ]
    for load in small_loads:
        load.start()

    pl.semaphore_wait(barrier, 23)

    def exchange(kind, src, dst):
        def copy(o):
            m = lax.rem(member + o, GROUP)
            return remote(src.at[m], dst.at[member], a_send.at[kind, o], a_recv.at[kind, o], at_member(m))

        def start():
            @pl.loop(1, GROUP)
            def _(o):
                copy(o).start()

        def arrive():
            @pl.loop(1, GROUP)
            def _(o):
                m = lax.rem(member + GROUP - o, GROUP)
                remote(src.at[m], dst.at[m], a_send.at[kind, o], a_recv.at[kind, o], at_member(m)).wait_recv()

        def sent():
            @pl.loop(1, GROUP)
            def _(o):
                copy(o).wait_send()

        return start, arrive, sent

    in_start, in_arrive, in_sent = exchange(0, x_ref, st.at[0])
    ct_start, ct_arrive, ct_sent = exchange(1, ct_ref, gst.at[SECTIONS])
    out_start, out_arrive, out_sent = exchange(2, st.at[SECTIONS], out_ref)
    gin_start, gin_arrive, gin_sent = exchange(3, gst.at[0], gin_ref)
    in_start()
    ct_start()

    acc_be[...] = jnp.zeros_like(acc_be)
    acc_br[...] = jnp.zeros_like(acc_br)
    acc_gg[...] = jnp.zeros_like(acc_gg)
    for load in small_loads:
        load.wait()
    sigma = jax.nn.sigmoid(gl_ref[...])

    load_we.wait()
    load_wr.wait()
    own_x.wait()
    in_arrive()

    def rows_of(s):
        return pl.ds(pl.multiple_of(s * 128, 128), 128)

    def share(kind, s):
        rows = rows_of(s)
        if kind == 0:
            src, dst = hid_t.at[:, rows], hid_s.at[:, rows]
        elif kind == 1:
            src, dst = norm_t.at[:, rows], norm_s.at[:, rows]
        elif kind == 2:
            cols = pl.ds(pl.multiple_of(256 * (1 - core), 256), 256)
            src, dst = gout.at[rows, cols], gout_s.at[rows]
        else:
            cols = pl.ds(pl.multiple_of(512 * (1 - core), 512), 512)
            src, dst = gpre.at[rows, cols], gpre_s.at[rows]
        return remote(src, dst, s_send.at[kind, s], s_recv.at[kind, s], sibling)

    def shared(kind):
        for s in range(SECTIONS):
            share(kind, s).wait_recv()

    def joined_of(s):
        lower = st[s, 0:8].reshape(128, 256).astype(F32)
        upper = st[s, 8:16].reshape(128, 256).astype(F32)
        return jnp.concatenate([lower, upper], axis=1)

    def forward(s):
        cols = pl.ds(pl.multiple_of(s * 128, 128), 128)
        joined = joined_of(s)
        centred = joined - jnp.mean(joined, axis=1, keepdims=True)
        inv_std = lax.rsqrt(jnp.mean(centred * centred, axis=1, keepdims=True) + EPSILON)
        normed = centred * inv_std
        nrm[s] = normed
        inv[s] = inv_std
        low = normed.astype(BF16)
        norm_t[:, cols] = low.T
        mixed = sigma * joined + br_ref[...]
        for h in range(4):
            hs = slice(256 * h, 256 * h + 256)
            pre = dot(low, we[:, hs], NN) + be_ref[:, hs]
            cdf = 0.5 + 0.5 * lax.erf(pre * math.sqrt(0.5))
            pdf = jnp.exp(-0.5 * pre * pre) * (1.0 / math.sqrt(2.0 * math.pi))
            dgelu[s, :, hs] = cdf + pre * pdf
            hidden = (pre * cdf).astype(BF16)
            hid_t[hs, cols] = hidden.T
            mixed = mixed + dot(hidden, wr[hs, :], NN)
        result = mixed.astype(BF16)
        for j in range(8):
            st[s + 1, 2 * j] = result[16 * j : 16 * j + 16, :256]
            st[s + 1, 2 * j + 1] = result[16 * j : 16 * j + 16, 256:]

    @pl.loop(0, SECTIONS)
    def _(s):
        forward(s)
        share(0, s).start()
        share(1, s).start()

    out_start()
    own_out = pltpu.make_async_copy(st.at[SECTIONS, member], out_ref.at[member], load_sem.at[4])
    own_out.start()

    own_ct.wait()
    ct_arrive()

    def upstream(s):
        lower = jnp.concatenate([gst[s + 1, 2 * j] for j in range(8)], axis=0)
        upper = jnp.concatenate([gst[s + 1, 2 * j + 1] for j in range(8)], axis=0)
        gout[rows_of(s), :] = jnp.concatenate([lower, upper], axis=1)

    def fold(v):
        return jnp.sum(v.reshape(16, 8, v.shape[1]), axis=0)

    def backward_hidden(s):
        grad = gout[rows_of(s), :]
        wide = grad.astype(F32)
        acc_br[...] += fold(wide)
        acc_gg[...] += fold(wide * joined_of(s))
        for h in range(4):
            hs = slice(256 * h, 256 * h + 256)
            pre = dot(grad, wr[hs, :], NT) * dgelu[s, :, hs]
            acc_be[:, hs] += fold(pre)
            gpre[rows_of(s), hs] = pre.astype(BF16)

    def backward_joined(s):
        wide = gout[rows_of(s), :].astype(F32)
        gnormed = dot(gpre[rows_of(s), :], we[...], NT)
        normed = nrm[s]
        mean = jnp.mean(gnormed, axis=1, keepdims=True)
        along = jnp.mean(gnormed * normed, axis=1, keepdims=True)
        result = (sigma * wide + inv[s] * (gnormed - mean - normed * along)).astype(BF16)
        gst[s, 0:8] = result[:, :256].reshape(8, 16, 256)
        gst[s, 8:16] = result[:, 256:].reshape(8, 16, 256)

    def product(k, hid, norm, grad, pre):
        if k < 2:
            return dot(hid[512 * k : 512 * k + 512, :], grad, NN)
        return dot(norm[...], pre, NN)

    def begin(k):
        grad = gout[:, pl.ds(pl.multiple_of(256 * core, 256), 256)] if k < 2 else None
        pre = gpre[:, pl.ds(pl.multiple_of(512 * core + 256 * (k - 2), 256), 256)] if k >= 2 else None
        own[k] = product(k, hid_t, norm_t, grad, pre)

    x_first = (True, False, True, False)

    def first(k, o):
        if x_first[k]:
            v = lax.rem(x + o, 4)
            src = part.at[k, v]
            device = at_x(v)
        else:
            v = lax.rem(y + o, 4)
            src = part.at[k, :, v]
            device = at_y(v)
        return remote(src, recv1.at[k, o], p_send.at[k, o], p_recv.at[k, o], device)

    def second(k, o):
        if x_first[k]:
            v = lax.rem(y + o, 4)
            device = at_y(v)
        else:
            v = lax.rem(x + o, 4)
            device = at_x(v)
        return remote(mid.at[k, v], recv2.at[k, o], q_send.at[k, o], q_recv.at[k, o], device)

    def scatter(k):
        grad = gout_s[...] if k < 2 else None
        pre = gpre_s[:, 256 * (k - 2) : 256 * (k - 1)] if k >= 2 else None
        total = own[k] + product(k, hid_s, norm_s, grad, pre)
        blocks = total.reshape((2, 16, 16, 256) if k < 2 else (4, 16, 8, 256))
        value = jnp.concatenate([blocks[i] for i in range(blocks.shape[0])], axis=1)
        part[k] = value.astype(BF16).reshape(4, 4, 32, 256)
        for o in range(1, 4):
            first(k, o).start()

    def scatter_again(k):
        for o in range(1, 4):
            first(k, o).wait_recv()
        mine = part[k, x] if x_first[k] else part[k, :, y]
        total = mine.astype(F32)
        for o in range(1, 4):
            total = total + recv1[k, o].astype(F32)
        mid[k] = total.astype(BF16)
        for o in range(1, 4):
            second(k, o).start()

    def reduced(k):
        for o in range(1, 4):
            second(k, o).wait_recv()
        total = (mid[k, y] if x_first[k] else mid[k, x]).astype(F32)
        for o in range(1, 4):
            total = total + recv2[k, o].astype(F32)
        return total

    def z_copy(half, o):
        v = lax.rem(z + o, 8)
        return remote(
            zsend.at[half, lax.rem(v, 4)], zrecv.at[half, z], z_send.at[half, o], z_recv.at[half, o], at_z(v)
        )

    def z_begin(half):
        for o in range(1, 8):
            z_copy(half, o).start()
        zrecv[half, z] = zsend[half, z_lo]

    def final_copy(half):
        return remote(fin.at[half], rfin.at[half], c_send.at[half], c_recv.at[half], sibling)

    def z_end(half):
        for o in range(1, 8):
            v = lax.rem(z + 8 - o, 8)
            remote(
                zsend.at[half, 0], zrecv.at[half, v], z_send.at[half, o], z_recv.at[half, o], at_z(v)
            ).wait_recv()
        total = zrecv[half, 0].astype(F32)
        for v in range(1, 8):
            total = total + zrecv[half, v].astype(F32)
        fin[half] = total * factor
        final_copy(half).start()

    def b_copy(n, o):
        sems = (b_send.at[n, o], b_recv.at[n, o])
        if n == 0:
            return remote(vec.at[1 - core], rvec, *sems, sibling)
        if n == 1:
            return remote(vx.at[x], vx.at[x], *sems, at_x(lax.rem(x + o, 4)))
        if n == 2:
            return remote(vy.at[y], vy.at[y], *sems, at_y(lax.rem(y + o, 4)))
        if n == 3:
            return remote(vz.at[z], vz.at[z], *sems, at_z(lax.rem(z + o, 8)))
        return remote(small.at[core], small.at[core], *sems, sibling)

    def b_arrive(n, o):
        sems = (b_send.at[n, o], b_recv.at[n, o])
        if n == 0:
            remote(vec.at[core], rvec, *sems, sibling).wait_recv()
        elif n == 1:
            v = lax.rem(x + 4 - o, 4)
            remote(vx.at[v], vx.at[v], *sems, at_x(v)).wait_recv()
        elif n == 2:
            v = lax.rem(y + 4 - o, 4)
            remote(vy.at[v], vy.at[v], *sems, at_y(v)).wait_recv()
        elif n == 3:
            v = lax.rem(z + 8 - o, 8)
            remote(vz.at[v], vz.at[v], *sems, at_z(v)).wait_recv()
        else:
            remote(small.at[1 - core], small.at[1 - core], *sems, sibling).wait_recv()

    B_COUNT = (range(0, 1), range(1, 4), range(1, 4), range(1, 8), range(0, 1))

    def b_begin(n):
        for o in B_COUNT[n]:
            b_copy(n, o).start()

    def b_end(n):
        for o in B_COUNT[n]:
            b_arrive(n, o)

    @pl.loop(0, SECTIONS - 1)
    def _(i):
        s = SECTIONS - 1 - i
        upstream(s)
        share(2, s).start()
        backward_hidden(s)
        share(3, s).start()
        backward_joined(s)

    def put(half, row, v):
        total = jnp.sum(v, axis=0, keepdims=True)
        for i in range(v.shape[1] // 128):
            vec[half, row + i : row + i + 1, :] = total[:, 128 * i : 128 * i + 128]

    upstream(0)
    share(2, 0).start()
    backward_hidden(0)
    share(3, 0).start()
    begin(0)
    begin(1)
    put(0, 0, acc_be[...])
    put(1, 0, acc_br[...])
    put(1, 4, acc_gg[...])
    b_begin(0)
    shared(0)
    shared(2)
    scatter(0)
    scatter(1)
    begin(2)
    begin(3)
    b_end(0)
    vx[x] = vec[core] + rvec[...]
    b_begin(1)
    shared(1)
    shared(3)
    scatter(2)
    scatter(3)
    backward_joined(0)
    gin_start()
    own_gin = pltpu.make_async_copy(gst.at[0, member], gin_ref.at[member], load_sem.at[5])
    own_gin.start()
    in_sent()
    ct_sent()
    out_sent()
    own_out.wait()
    out_arrive()
    scatter_again(0)
    scatter_again(1)
    b_end(1)
    vy[y] = (vx[0] + vx[1]) + (vx[2] + vx[3])
    b_begin(2)
    scatter_again(2)
    scatter_again(3)
    for k in range(2):
        block = reduced(k)
        for i in range(2):
            zsend[0, 2 * k + i] = block[16 * i : 16 * i + 16].astype(BF16)
    z_begin(0)
    b_end(2)
    vz[z] = (vy[0] + vy[1]) + (vy[2] + vy[3])
    b_begin(3)
    left = reduced(2)
    right = reduced(3)
    for i in range(4):
        rows = slice(8 * i, 8 * i + 8)
        zsend[1, i] = jnp.concatenate([left[rows], right[rows]], axis=0).astype(BF16)
    z_begin(1)
    z_end(0)
    b_end(3)
    total = vz[0]
    for v in range(1, 8):
        total = total + vz[v]
    small[core] = total * factor
    b_begin(4)
    own_gin.wait()
    gin_arrive()
    gin_sent()
    for k in range(4):
        for i in range(SECTIONS):
            share(k, i).wait_send()
        for o in range(1, 4):
            first(k, o).wait_send()
            second(k, o).wait_send()
    z_end(1)

    def place(half, value, who):
        if half == 0:
            o_wr[:, pl.ds(pl.multiple_of(256 * who, 256), 256)] = value
        else:
            for i in range(2):
                o_we[:, pl.ds(pl.multiple_of(512 * who + 256 * i, 256), 256)] = value[8 * i : 8 * i + 8]

    for half in range(2):
        place(half, fin[half], core)
    for half in range(2):
        final_copy(half).wait_recv()
        place(half, rfin[half], 1 - core)
    b_end(4)
    for i in range(8):
        o_be[:, 128 * i : 128 * i + 128] = small[0, i : i + 1]
    for i in range(4):
        cols = slice(128 * i, 128 * i + 128)
        o_br[:, cols] = small[1, i : i + 1]
        sg = sigma[:, cols]
        o_gg[:, cols] = small[1, 4 + i : 5 + i] * (sg * (1.0 - sg))

    for half in range(2):
        final_copy(half).wait_send()
        for o in range(1, 8):
            z_copy(half, o).wait_send()
    for n in range(5):
        for o in B_COUNT[n]:
            b_copy(n, o).wait_send()


def finish(*refs):
    n = len(refs) // 2
    copies = [pltpu.make_async_copy(refs[i], refs[n + i], refs[2 * n].at[i]) for i in range(n)]
    for copy in copies:
        copy.start()
    for copy in copies:
        copy.wait()


def hand_on(arrays):
    n = len(arrays)
    return pl.pallas_call(
        finish,
        out_shape=tuple(jax.ShapeDtypeStruct(a.shape, a.dtype) for a in arrays),
        in_specs=[pl.BlockSpec(memory_space=pl.ANY)] * n,
        out_specs=(pl.BlockSpec(memory_space=pltpu.HBM),) * n,
        scratch_shapes=[pltpu.SemaphoreType.DMA((n,))],
        compiler_params=pltpu.CompilerParams(vmem_limit_bytes=1024 * 1024),
    )(*arrays)


def body(inputs, w_expand, b_expand, w_reduce, b_reduce, gate_logit, cotangent):
    rows, width = inputs.shape[1:]
    hidden = w_expand.shape[1]
    block = rows // GROUP
    factor = 1.0 / math.sqrt(lax.axis_size("rep") * lax.axis_size("ctx") * rows)
    any_spec = pl.BlockSpec(memory_space=pl.ANY)
    vmem = pl.BlockSpec(memory_space=pltpu.VMEM)
    dma = pltpu.SemaphoreType.DMA
    results = pl.pallas_call(
        functools.partial(kernel, factor),
        out_shape=(
            jax.ShapeDtypeStruct((GROUP, block, width), BF16),
            jax.ShapeDtypeStruct((GROUP, block, width), BF16),
            jax.ShapeDtypeStruct((8, 1024), F32),
            jax.ShapeDtypeStruct((1, 1024), F32),
            jax.ShapeDtypeStruct((16, 512), F32),
            jax.ShapeDtypeStruct((1, 512), F32),
            jax.ShapeDtypeStruct((1, 512), F32),
        ),
        in_specs=[pl.BlockSpec(memory_space=pltpu.HBM)] * 7,
        out_specs=(any_spec, any_spec, vmem, vmem, vmem, vmem, vmem),
        scratch_shapes=[
            pltpu.VMEM((512, 1024), BF16),
            pltpu.VMEM((1024, 512), BF16),
            pltpu.VMEM((1, 1024), F32),
            pltpu.VMEM((1, 512), F32),
            pltpu.VMEM((1, 512), F32),
            pltpu.VMEM((SECTIONS + 1, 16, 16, 256), BF16),
            pltpu.VMEM((SECTIONS + 1, 16, 16, 256), BF16),
            pltpu.VMEM((SECTIONS, 128, 512), F32),
            pltpu.VMEM((SECTIONS, 128, 1), F32),
            pltpu.VMEM((512, 512), BF16),
            pltpu.VMEM((1024, 512), BF16),
            pltpu.VMEM((SECTIONS, 128, 1024), F32),
            pltpu.VMEM((512, 512), BF16),
            pltpu.VMEM((512, 1024), BF16),
            pltpu.VMEM((1024, 512), BF16),
            pltpu.VMEM((512, 512), BF16),
            pltpu.VMEM((512, 256), BF16),
            pltpu.VMEM((512, 512), BF16),
            pltpu.VMEM((4, 512, 256), F32),
            pltpu.VMEM((4, 4, 4, 32, 256), BF16),
            pltpu.VMEM((4, 4, 4, 32, 256), BF16),
            pltpu.VMEM((4, 4, 32, 256), BF16),
            pltpu.VMEM((4, 4, 32, 256), BF16),
            pltpu.VMEM((2, 4, 16, 256), BF16),
            pltpu.VMEM((2, 8, 16, 256), BF16),
            pltpu.VMEM((2, 16, 256), F32),
            pltpu.VMEM((2, 16, 256), F32),
            pltpu.VMEM((8, 1024), F32),
            pltpu.VMEM((8, 512), F32),
            pltpu.VMEM((8, 512), F32),
            pltpu.VMEM((2, 8, 128), F32),
            pltpu.VMEM((8, 128), F32),
            pltpu.VMEM((4, 8, 128), F32),
            pltpu.VMEM((4, 8, 128), F32),
            pltpu.VMEM((8, 8, 128), F32),
            pltpu.VMEM((2, 8, 128), F32),
            dma((9,)),
            dma((4, 16)),
            dma((4, 16)),
            dma((2,)),
            dma((2,)),
            dma((4, SECTIONS)),
            dma((4, SECTIONS)),
            dma((4, 4)),
            dma((4, 4)),
            dma((4, 4)),
            dma((4, 4)),
            dma((2, 8)),
            dma((2, 8)),
            dma((5, 8)),
            dma((5, 8)),
        ],
        compiler_params=pltpu.CompilerParams(collective_id=0, has_side_effects=True, vmem_limit_bytes=24 * 1024 * 1024),
    )(
        *(
            pltpu.with_memory_space_constraint(value, pltpu.HBM)
            for value in (
                inputs.reshape(GROUP, block, width),
                w_expand,
                b_expand.reshape(1, hidden),
                w_reduce,
                b_reduce.reshape(1, 2 * width),
                gate_logit.reshape(1, 2 * width),
                cotangent.reshape(GROUP, block, width),
            )
        )
    )
    out, gin, g_we, g_be, g_wr, g_br, g_gg = hand_on(results)
    return (
        out.reshape(inputs.shape),
        gin.reshape(inputs.shape),
        g_we,
        g_be.reshape(hidden),
        g_wr,
        g_br.reshape(2 * width),
        g_gg.reshape(2 * width),
    )


def solution(mesh):
    return jax.shard_map(
        body,
        mesh=mesh,
        in_specs=(P("rep", "ctx", None), P(), P(), P(), P(), P(), P("rep", "ctx", None)),
        out_specs=(
            P("rep", "ctx", None),
            P("rep", "ctx", None),
            P("ctx", None),
            P(),
            P("ctx", None),
            P(),
            P(),
        ),
        check_vma=False,
    )
```

```python
import functools
import math

import jax
import jax.numpy as jnp
from jax import lax
from jax.experimental import pallas as pl
from jax.experimental.pallas import tpu as pltpu
from jax.sharding import PartitionSpec as P

MESH = pl.DeviceIdType.MESH
F32 = jnp.float32
BF16 = jnp.bfloat16
EPSILON = 1e-05
SECTIONS = 4
GROUP = 16


def dot(a, b, dims):
    return lax.dot_general(a, b, (dims, ((), ())), preferred_element_type=F32)


NN = ((1,), (0,))
NT = ((1,), (1,))


def kernel(
    factor,
    x_ref,
    we_hbm,
    be_hbm,
    wr_hbm,
    br_hbm,
    gl_hbm,
    ct_ref,
    out_ref,
    gin_ref,
    o_we,
    o_be,
    o_wr,
    o_br,
    o_gg,
    we,
    wr,
    be_ref,
    br_ref,
    gl_ref,
    st,
    gst,
    nrm,
    inv,
    norm_t,
    hid_t,
    dgelu,
    gout,
    gpre,
    hid_s,
    norm_s,
    gout_s,
    gpre_s,
    own,
    part,
    recv1,
    mid,
    recv2,
    zsend,
    zrecv,
    fin,
    rfin,
    acc_be,
    acc_br,
    acc_gg,
    vec,
    rvec,
    vx,
    vy,
    vz,
    small,
    load_sem,
    a_send,
    a_recv,
    c_send,
    c_recv,
    s_send,
    s_recv,
    p_send,
    p_recv,
    q_send,
    q_recv,
    z_send,
    z_recv,
    b_send,
    b_recv,
):
    ctx = lax.axis_index("ctx")
    rep = lax.axis_index("rep")
    y = lax.rem(ctx, 4)
    member = lax.div(ctx, 4)
    x = lax.rem(member, 4)
    z_lo = lax.div(member, 4)
    core = lax.rem(rep, 2)
    z_hi = lax.div(rep, 2)
    z = z_hi * 4 + z_lo

    def at_member(m):
        return (m * 4 + y, rep)

    def at_x(v):
        return (z_lo * 16 + v * 4 + y, rep)

    def at_y(v):
        return (member * 4 + v, rep)

    def at_z(v):
        return (lax.rem(v, 4) * 16 + x * 4 + y, lax.div(v, 4) * 2 + core)

    sibling = (ctx, z_hi * 2 + 1 - core)

    def remote(src, dst, send, recv, device):
        return pltpu.make_async_remote_copy(
            src_ref=src, dst_ref=dst, send_sem=send, recv_sem=recv, device_id=device, device_id_type=MESH
        )

    barrier = pltpu.get_barrier_semaphore()

    def hello(device):
        pl.semaphore_signal(barrier, inc=1, device_id=device, device_id_type=MESH)

    @pl.loop(1, GROUP)
    def _(o):
        hello(at_member(lax.rem(member + o, GROUP)))

    for o in range(1, 4):
        hello(at_y(lax.rem(y + o, 4)))
    for v in range(4):
        hello(at_z((1 - z_hi) * 4 + v))
    hello(sibling)
    load_we = pltpu.make_async_copy(we_hbm, we, load_sem.at[0])
    load_wr = pltpu.make_async_copy(wr_hbm, wr, load_sem.at[1])
    own_x = pltpu.make_async_copy(x_ref.at[member], st.at[0, member], load_sem.at[2])
    own_ct = pltpu.make_async_copy(ct_ref.at[member], gst.at[SECTIONS, member], load_sem.at[3])
    own_x.start()
    load_we.start()
    load_wr.start()
    own_ct.start()
    small_loads = [
        pltpu.make_async_copy(a, b, load_sem.at[6 + i])
        for i, (a, b) in enumerate(((be_hbm, be_ref), (br_hbm, br_ref), (gl_hbm, gl_ref)))
    ]
    for load in small_loads:
        load.start()

    pl.semaphore_wait(barrier, 23)

    def exchange(kind, src, dst):
        def copy(o):
            m = lax.rem(member + o, GROUP)
            return remote(src.at[m], dst.at[member], a_send.at[kind, o], a_recv.at[kind, o], at_member(m))

        def start():
            @pl.loop(1, GROUP)
            def _(o):
                copy(o).start()

        def arrive():
            @pl.loop(1, GROUP)
            def _(o):
                m = lax.rem(member + GROUP - o, GROUP)
                remote(src.at[m], dst.at[m], a_send.at[kind, o], a_recv.at[kind, o], at_member(m)).wait_recv()

        def sent():
            @pl.loop(1, GROUP)
            def _(o):
                copy(o).wait_send()

        return start, arrive, sent

    in_start, in_arrive, in_sent = exchange(0, x_ref, st.at[0])
    ct_start, ct_arrive, ct_sent = exchange(1, ct_ref, gst.at[SECTIONS])
    out_start, out_arrive, out_sent = exchange(2, st.at[SECTIONS], out_ref)
    gin_start, gin_arrive, gin_sent = exchange(3, gst.at[0], gin_ref)
    in_start()
    ct_start()

    acc_be[...] = jnp.zeros_like(acc_be)
    acc_br[...] = jnp.zeros_like(acc_br)
    acc_gg[...] = jnp.zeros_like(acc_gg)
    for load in small_loads:
        load.wait()
    sigma = jax.nn.sigmoid(gl_ref[...])

    load_we.wait()
    load_wr.wait()
    own_x.wait()
    in_arrive()

    def rows_of(s):
        return pl.ds(pl.multiple_of(s * 128, 128), 128)

    def share(kind, s):
        rows = rows_of(s)
        if kind == 0:
            src, dst = hid_t.at[:, rows], hid_s.at[:, rows]
        elif kind == 1:
            src, dst = norm_t.at[:, rows], norm_s.at[:, rows]
        elif kind == 2:
            cols = pl.ds(pl.multiple_of(256 * (1 - core), 256), 256)
            src, dst = gout.at[rows, cols], gout_s.at[rows]
        else:
            cols = pl.ds(pl.multiple_of(512 * (1 - core), 512), 512)
            src, dst = gpre.at[rows, cols], gpre_s.at[rows]
        return remote(src, dst, s_send.at[kind, s], s_recv.at[kind, s], sibling)

    def shared(kind):
        for s in range(SECTIONS):
            share(kind, s).wait_recv()

    def joined_of(s):
        lower = st[s, 0:8].reshape(128, 256).astype(F32)
        upper = st[s, 8:16].reshape(128, 256).astype(F32)
        return jnp.concatenate([lower, upper], axis=1)

    def forward(s):
        cols = pl.ds(pl.multiple_of(s * 128, 128), 128)
        joined = joined_of(s)
        centred = joined - jnp.mean(joined, axis=1, keepdims=True)
        inv_std = lax.rsqrt(jnp.mean(centred * centred, axis=1, keepdims=True) + EPSILON)
        normed = centred * inv_std
        nrm[s] = normed
        inv[s] = inv_std
        low = normed.astype(BF16)
        norm_t[:, cols] = low.T
        mixed = sigma * joined + br_ref[...]
        for h in range(4):
            hs = slice(256 * h, 256 * h + 256)
            pre = dot(low, we[:, hs], NN) + be_ref[:, hs]
            cdf = 0.5 + 0.5 * lax.erf(pre * math.sqrt(0.5))
            pdf = jnp.exp(-0.5 * pre * pre) * (1.0 / math.sqrt(2.0 * math.pi))
            dgelu[s, :, hs] = cdf + pre * pdf
            hidden = (pre * cdf).astype(BF16)
            hid_t[hs, cols] = hidden.T
            mixed = mixed + dot(hidden, wr[hs, :], NN)
        result = mixed.astype(BF16)
        for j in range(8):
            st[s + 1, 2 * j] = result[16 * j : 16 * j + 16, :256]
            st[s + 1, 2 * j + 1] = result[16 * j : 16 * j + 16, 256:]

    @pl.loop(0, SECTIONS)
    def _(s):
        forward(s)
        share(0, s).start()
        share(1, s).start()

    out_start()
    own_out = pltpu.make_async_copy(st.at[SECTIONS, member], out_ref.at[member], load_sem.at[4])
    own_out.start()

    own_ct.wait()
    ct_arrive()

    def upstream(s):
        lower = jnp.concatenate([gst[s + 1, 2 * j] for j in range(8)], axis=0)
        upper = jnp.concatenate([gst[s + 1, 2 * j + 1] for j in range(8)], axis=0)
        gout[rows_of(s), :] = jnp.concatenate([lower, upper], axis=1)

    def fold(v):
        return jnp.sum(v.reshape(16, 8, v.shape[1]), axis=0)

    def backward_hidden(s):
        grad = gout[rows_of(s), :]
        wide = grad.astype(F32)
        acc_br[...] += fold(wide)
        acc_gg[...] += fold(wide * joined_of(s))
        for h in range(4):
            hs = slice(256 * h, 256 * h + 256)
            pre = dot(grad, wr[hs, :], NT) * dgelu[s, :, hs]
            acc_be[:, hs] += fold(pre)
            gpre[rows_of(s), hs] = pre.astype(BF16)

    def backward_joined(s):
        wide = gout[rows_of(s), :].astype(F32)
        gnormed = dot(gpre[rows_of(s), :], we[...], NT)
        normed = nrm[s]
        mean = jnp.mean(gnormed, axis=1, keepdims=True)
        along = jnp.mean(gnormed * normed, axis=1, keepdims=True)
        result = (sigma * wide + inv[s] * (gnormed - mean - normed * along)).astype(BF16)
        gst[s, 0:8] = result[:, :256].reshape(8, 16, 256)
        gst[s, 8:16] = result[:, 256:].reshape(8, 16, 256)

    def product(k, hid, norm, grad, pre):
        if k < 2:
            return dot(hid[512 * k : 512 * k + 512, :], grad, NN)
        return dot(norm[...], pre, NN)

    def begin(k):
        grad = gout[:, pl.ds(pl.multiple_of(256 * core, 256), 256)] if k < 2 else None
        pre = gpre[:, pl.ds(pl.multiple_of(512 * core + 256 * (k - 2), 256), 256)] if k >= 2 else None
        own[k] = product(k, hid_t, norm_t, grad, pre)

    x_first = (True, False, True, False)

    def first(k, o):
        if x_first[k]:
            v = lax.rem(x + o, 4)
            src = part.at[k, v]
            device = at_x(v)
        else:
            v = lax.rem(y + o, 4)
            src = part.at[k, :, v]
            device = at_y(v)
        return remote(src, recv1.at[k, o], p_send.at[k, o], p_recv.at[k, o], device)

    def second(k, o):
        if x_first[k]:
            v = lax.rem(y + o, 4)
            device = at_y(v)
        else:
            v = lax.rem(x + o, 4)
            device = at_x(v)
        return remote(mid.at[k, v], recv2.at[k, o], q_send.at[k, o], q_recv.at[k, o], device)

    def scatter(k):
        grad = gout_s[...] if k < 2 else None
        pre = gpre_s[:, 256 * (k - 2) : 256 * (k - 1)] if k >= 2 else None
        total = own[k] + product(k, hid_s, norm_s, grad, pre)
        blocks = total.reshape((2, 16, 16, 256) if k < 2 else (4, 16, 8, 256))
        value = jnp.concatenate([blocks[i] for i in range(blocks.shape[0])], axis=1)
        part[k] = value.astype(BF16).reshape(4, 4, 32, 256)
        for o in (2, 1, 3):
            first(k, o).start()

    def scatter_again(k):
        for o in range(1, 4):
            first(k, o).wait_recv()
        mine = part[k, x] if x_first[k] else part[k, :, y]
        total = mine.astype(F32)
        for o in range(1, 4):
            total = total + recv1[k, o].astype(F32)
        mid[k] = total.astype(BF16)
        for o in (2, 1, 3):
            second(k, o).start()

    def reduced(k):
        for o in range(1, 4):
            second(k, o).wait_recv()
        total = (mid[k, y] if x_first[k] else mid[k, x]).astype(F32)
        for o in range(1, 4):
            total = total + recv2[k, o].astype(F32)
        return total

    def z_copy(half, o):
        v = lax.rem(z + o, 8)
        return remote(
            zsend.at[half, lax.rem(v, 4)], zrecv.at[half, z], z_send.at[half, o], z_recv.at[half, o], at_z(v)
        )

    def z_begin(half):
        for o in (4, 3, 5, 2, 6, 1, 7):
            z_copy(half, o).start()
        zrecv[half, z] = zsend[half, z_lo]

    def final_copy(half):
        return remote(fin.at[half], rfin.at[half], c_send.at[half], c_recv.at[half], sibling)

    def z_end(half):
        for o in range(1, 8):
            v = lax.rem(z + 8 - o, 8)
            remote(
                zsend.at[half, 0], zrecv.at[half, v], z_send.at[half, o], z_recv.at[half, o], at_z(v)
            ).wait_recv()
        total = zrecv[half, 0].astype(F32)
        for v in range(1, 8):
            total = total + zrecv[half, v].astype(F32)
        fin[half] = total * factor
        final_copy(half).start()

    def b_copy(n, o):
        sems = (b_send.at[n, o], b_recv.at[n, o])
        if n == 0:
            return remote(vec.at[1 - core], rvec, *sems, sibling)
        if n == 1:
            return remote(vx.at[x], vx.at[x], *sems, at_x(lax.rem(x + o, 4)))
        if n == 2:
            return remote(vy.at[y], vy.at[y], *sems, at_y(lax.rem(y + o, 4)))
        if n == 3:
            return remote(vz.at[z], vz.at[z], *sems, at_z(lax.rem(z + o, 8)))
        return remote(small.at[core], small.at[core], *sems, sibling)

    def b_arrive(n, o):
        sems = (b_send.at[n, o], b_recv.at[n, o])
        if n == 0:
            remote(vec.at[core], rvec, *sems, sibling).wait_recv()
        elif n == 1:
            v = lax.rem(x + 4 - o, 4)
            remote(vx.at[v], vx.at[v], *sems, at_x(v)).wait_recv()
        elif n == 2:
            v = lax.rem(y + 4 - o, 4)
            remote(vy.at[v], vy.at[v], *sems, at_y(v)).wait_recv()
        elif n == 3:
            v = lax.rem(z + 8 - o, 8)
            remote(vz.at[v], vz.at[v], *sems, at_z(v)).wait_recv()
        else:
            remote(small.at[1 - core], small.at[1 - core], *sems, sibling).wait_recv()

    B_COUNT = (range(0, 1), range(1, 4), range(1, 4), range(1, 8), range(0, 1))

    def b_begin(n):
        for o in B_COUNT[n]:
            b_copy(n, o).start()

    def b_end(n):
        for o in B_COUNT[n]:
            b_arrive(n, o)

    @pl.loop(0, SECTIONS - 1)
    def _(i):
        s = SECTIONS - 1 - i
        upstream(s)
        share(2, s).start()
        backward_hidden(s)
        share(3, s).start()
        backward_joined(s)

    def put(half, row, v):
        total = jnp.sum(v, axis=0, keepdims=True)
        for i in range(v.shape[1] // 128):
            vec[half, row + i : row + i + 1, :] = total[:, 128 * i : 128 * i + 128]

    upstream(0)
    share(2, 0).start()
    backward_hidden(0)
    share(3, 0).start()
    begin(0)
    begin(1)
    put(0, 0, acc_be[...])
    put(1, 0, acc_br[...])
    put(1, 4, acc_gg[...])
    b_begin(0)
    shared(0)
    shared(2)
    scatter(0)
    scatter(1)
    begin(2)
    begin(3)
    b_end(0)
    vx[x] = vec[core] + rvec[...]
    b_begin(1)
    shared(1)
    shared(3)
    scatter(2)
    scatter(3)
    backward_joined(0)
    in_sent()
    ct_sent()
    out_sent()
    own_out.wait()
    out_arrive()
    scatter_again(0)
    scatter_again(1)
    b_end(1)
    vy[y] = (vx[0] + vx[1]) + (vx[2] + vx[3])
    b_begin(2)
    scatter_again(2)
    scatter_again(3)
    gin_start()
    own_gin = pltpu.make_async_copy(gst.at[0, member], gin_ref.at[member], load_sem.at[5])
    own_gin.start()
    for k in range(2):
        block = reduced(k)
        for i in range(2):
            zsend[0, 2 * k + i] = block[16 * i : 16 * i + 16].astype(BF16)
    z_begin(0)
    b_end(2)
    vz[z] = (vy[0] + vy[1]) + (vy[2] + vy[3])
    b_begin(3)
    left = reduced(2)
    right = reduced(3)
    for i in range(4):
        rows = slice(8 * i, 8 * i + 8)
        zsend[1, i] = jnp.concatenate([left[rows], right[rows]], axis=0).astype(BF16)
    z_begin(1)
    z_end(0)
    b_end(3)
    total = vz[0]
    for v in range(1, 8):
        total = total + vz[v]
    small[core] = total * factor
    b_begin(4)
    own_gin.wait()
    gin_arrive()
    gin_sent()
    for k in range(4):
        for i in range(SECTIONS):
            share(k, i).wait_send()
        for o in range(1, 4):
            first(k, o).wait_send()
            second(k, o).wait_send()
    z_end(1)

    def place(half, value, who):
        if half == 0:
            o_wr[:, pl.ds(pl.multiple_of(256 * who, 256), 256)] = value
        else:
            for i in range(2):
                o_we[:, pl.ds(pl.multiple_of(512 * who + 256 * i, 256), 256)] = value[8 * i : 8 * i + 8]

    for half in range(2):
        place(half, fin[half], core)
    for half in range(2):
        final_copy(half).wait_recv()
        place(half, rfin[half], 1 - core)
    b_end(4)
    for i in range(8):
        o_be[:, 128 * i : 128 * i + 128] = small[0, i : i + 1]
    for i in range(4):
        cols = slice(128 * i, 128 * i + 128)
        o_br[:, cols] = small[1, i : i + 1]
        sg = sigma[:, cols]
        o_gg[:, cols] = small[1, 4 + i : 5 + i] * (sg * (1.0 - sg))

    for half in range(2):
        final_copy(half).wait_send()
        for o in range(1, 8):
            z_copy(half, o).wait_send()
    for n in range(5):
        for o in B_COUNT[n]:
            b_copy(n, o).wait_send()


def finish(*refs):
    n = len(refs) // 2
    copies = [pltpu.make_async_copy(refs[i], refs[n + i], refs[2 * n].at[i]) for i in range(n)]
    for copy in copies:
        copy.start()
    for copy in copies:
        copy.wait()


def hand_on(arrays):
    n = len(arrays)
    return pl.pallas_call(
        finish,
        out_shape=tuple(jax.ShapeDtypeStruct(a.shape, a.dtype) for a in arrays),
        in_specs=[pl.BlockSpec(memory_space=pl.ANY)] * n,
        out_specs=(pl.BlockSpec(memory_space=pltpu.HBM),) * n,
        scratch_shapes=[pltpu.SemaphoreType.DMA((n,))],
        compiler_params=pltpu.CompilerParams(vmem_limit_bytes=1024 * 1024),
    )(*arrays)


def body(inputs, w_expand, b_expand, w_reduce, b_reduce, gate_logit, cotangent):
    rows, width = inputs.shape[1:]
    hidden = w_expand.shape[1]
    block = rows // GROUP
    factor = 1.0 / math.sqrt(lax.axis_size("rep") * lax.axis_size("ctx") * rows)
    any_spec = pl.BlockSpec(memory_space=pl.ANY)
    vmem = pl.BlockSpec(memory_space=pltpu.VMEM)
    dma = pltpu.SemaphoreType.DMA
    results = pl.pallas_call(
        functools.partial(kernel, factor),
        out_shape=(
            jax.ShapeDtypeStruct((GROUP, block, width), BF16),
            jax.ShapeDtypeStruct((GROUP, block, width), BF16),
            jax.ShapeDtypeStruct((8, 1024), F32),
            jax.ShapeDtypeStruct((1, 1024), F32),
            jax.ShapeDtypeStruct((16, 512), F32),
            jax.ShapeDtypeStruct((1, 512), F32),
            jax.ShapeDtypeStruct((1, 512), F32),
        ),
        in_specs=[pl.BlockSpec(memory_space=pltpu.HBM)] * 7,
        out_specs=(any_spec, any_spec, vmem, vmem, vmem, vmem, vmem),
        scratch_shapes=[
            pltpu.VMEM((512, 1024), BF16),
            pltpu.VMEM((1024, 512), BF16),
            pltpu.VMEM((1, 1024), F32),
            pltpu.VMEM((1, 512), F32),
            pltpu.VMEM((1, 512), F32),
            pltpu.VMEM((SECTIONS + 1, 16, 16, 256), BF16),
            pltpu.VMEM((SECTIONS + 1, 16, 16, 256), BF16),
            pltpu.VMEM((SECTIONS, 128, 512), F32),
            pltpu.VMEM((SECTIONS, 128, 1), F32),
            pltpu.VMEM((512, 512), BF16),
            pltpu.VMEM((1024, 512), BF16),
            pltpu.VMEM((SECTIONS, 128, 1024), F32),
            pltpu.VMEM((512, 512), BF16),
            pltpu.VMEM((512, 1024), BF16),
            pltpu.VMEM((1024, 512), BF16),
            pltpu.VMEM((512, 512), BF16),
            pltpu.VMEM((512, 256), BF16),
            pltpu.VMEM((512, 512), BF16),
            pltpu.VMEM((4, 512, 256), F32),
            pltpu.VMEM((4, 4, 4, 32, 256), BF16),
            pltpu.VMEM((4, 4, 4, 32, 256), BF16),
            pltpu.VMEM((4, 4, 32, 256), BF16),
            pltpu.VMEM((4, 4, 32, 256), BF16),
            pltpu.VMEM((2, 4, 16, 256), BF16),
            pltpu.VMEM((2, 8, 16, 256), BF16),
            pltpu.VMEM((2, 16, 256), F32),
            pltpu.VMEM((2, 16, 256), F32),
            pltpu.VMEM((8, 1024), F32),
            pltpu.VMEM((8, 512), F32),
            pltpu.VMEM((8, 512), F32),
            pltpu.VMEM((2, 8, 128), F32),
            pltpu.VMEM((8, 128), F32),
            pltpu.VMEM((4, 8, 128), F32),
            pltpu.VMEM((4, 8, 128), F32),
            pltpu.VMEM((8, 8, 128), F32),
            pltpu.VMEM((2, 8, 128), F32),
            dma((9,)),
            dma((4, 16)),
            dma((4, 16)),
            dma((2,)),
            dma((2,)),
            dma((4, SECTIONS)),
            dma((4, SECTIONS)),
            dma((4, 4)),
            dma((4, 4)),
            dma((4, 4)),
            dma((4, 4)),
            dma((2, 8)),
            dma((2, 8)),
            dma((5, 8)),
            dma((5, 8)),
        ],
        compiler_params=pltpu.CompilerParams(collective_id=0, has_side_effects=True, vmem_limit_bytes=24 * 1024 * 1024),
    )(
        *(
            pltpu.with_memory_space_constraint(value, pltpu.HBM)
            for value in (
                inputs.reshape(GROUP, block, width),
                w_expand,
                b_expand.reshape(1, hidden),
                w_reduce,
                b_reduce.reshape(1, 2 * width),
                gate_logit.reshape(1, 2 * width),
                cotangent.reshape(GROUP, block, width),
            )
        )
    )
    out, gin, g_we, g_be, g_wr, g_br, g_gg = hand_on(results)
    return (
        out.reshape(inputs.shape),
        gin.reshape(inputs.shape),
        g_we,
        g_be.reshape(hidden),
        g_wr,
        g_br.reshape(2 * width),
        g_gg.reshape(2 * width),
    )


def solution(mesh):
    return jax.shard_map(
        body,
        mesh=mesh,
        in_specs=(P("rep", "ctx", None), P(), P(), P(), P(), P(), P("rep", "ctx", None)),
        out_specs=(
            P("rep", "ctx", None),
            P("rep", "ctx", None),
            P("ctx", None),
            P(),
            P("ctx", None),
            P(),
            P(),
        ),
        check_vma=False,
    )
```

```python
import functools
import math

import jax
import jax.numpy as jnp
from jax import lax
from jax.experimental import pallas as pl
from jax.experimental.pallas import tpu as pltpu
from jax.sharding import PartitionSpec as P

MESH = pl.DeviceIdType.MESH
F32 = jnp.float32
BF16 = jnp.bfloat16
EPSILON = 1e-05
SECTIONS = 4
GROUP = 16


def dot(a, b, dims):
    return lax.dot_general(a, b, (dims, ((), ())), preferred_element_type=F32)


NN = ((1,), (0,))
NT = ((1,), (1,))


def kernel(
    factor,
    x_ref,
    we_hbm,
    be_hbm,
    wr_hbm,
    br_hbm,
    gl_hbm,
    ct_ref,
    out_ref,
    gin_ref,
    o_we,
    o_be,
    o_wr,
    o_br,
    o_gg,
    we,
    wr,
    be_ref,
    br_ref,
    gl_ref,
    st,
    gst,
    nrm,
    inv,
    norm_t,
    hid_t,
    dgelu,
    gout,
    gpre,
    hid_s,
    norm_s,
    gout_s,
    gpre_s,
    own,
    part,
    recv1,
    mid,
    recv2,
    zsend,
    zrecv,
    fin,
    rfin,
    acc_be,
    acc_br,
    acc_gg,
    vec,
    rvec,
    vx,
    vy,
    vz,
    small,
    load_sem,
    a_send,
    a_recv,
    c_send,
    c_recv,
    s_send,
    s_recv,
    p_send,
    p_recv,
    q_send,
    q_recv,
    z_send,
    z_recv,
    b_send,
    b_recv,
):
    ctx = lax.axis_index("ctx")
    rep = lax.axis_index("rep")
    y = lax.rem(ctx, 4)
    member = lax.div(ctx, 4)
    x = lax.rem(member, 4)
    z_lo = lax.div(member, 4)
    core = lax.rem(rep, 2)
    z_hi = lax.div(rep, 2)
    z = z_hi * 4 + z_lo

    def at_member(m):
        return (m * 4 + y, rep)

    def at_x(v):
        return (z_lo * 16 + v * 4 + y, rep)

    def at_y(v):
        return (member * 4 + v, rep)

    def at_z(v):
        return (lax.rem(v, 4) * 16 + x * 4 + y, lax.div(v, 4) * 2 + core)

    sibling = (ctx, z_hi * 2 + 1 - core)

    def remote(src, dst, send, recv, device):
        return pltpu.make_async_remote_copy(
            src_ref=src, dst_ref=dst, send_sem=send, recv_sem=recv, device_id=device, device_id_type=MESH
        )

    barrier = pltpu.get_barrier_semaphore()

    def hello(device):
        pl.semaphore_signal(barrier, inc=1, device_id=device, device_id_type=MESH)

    @pl.loop(1, GROUP)
    def _(o):
        hello(at_member(lax.rem(member + o, GROUP)))

    for o in range(1, 4):
        hello(at_y(lax.rem(y + o, 4)))
    for v in range(4):
        hello(at_z((1 - z_hi) * 4 + v))
    hello(sibling)
    load_we = pltpu.make_async_copy(we_hbm, we, load_sem.at[0])
    load_wr = pltpu.make_async_copy(wr_hbm, wr, load_sem.at[1])
    own_x = pltpu.make_async_copy(x_ref.at[member], st.at[0, member], load_sem.at[2])
    own_ct = pltpu.make_async_copy(ct_ref.at[member], gst.at[SECTIONS, member], load_sem.at[3])
    own_x.start()
    load_we.start()
    load_wr.start()
    own_ct.start()
    small_loads = [
        pltpu.make_async_copy(a, b, load_sem.at[6 + i])
        for i, (a, b) in enumerate(((be_hbm, be_ref), (br_hbm, br_ref), (gl_hbm, gl_ref)))
    ]
    for load in small_loads:
        load.start()

    pl.semaphore_wait(barrier, 23)

    def exchange(kind, src, dst):
        def copy(o):
            m = lax.rem(member + o, GROUP)
            return remote(src.at[m], dst.at[member], a_send.at[kind, o], a_recv.at[kind, o], at_member(m))

        def start():
            @pl.loop(1, GROUP)
            def _(o):
                copy(o).start()

        def arrive():
            @pl.loop(1, GROUP)
            def _(o):
                m = lax.rem(member + GROUP - o, GROUP)
                remote(src.at[m], dst.at[m], a_send.at[kind, o], a_recv.at[kind, o], at_member(m)).wait_recv()

        def sent():
            @pl.loop(1, GROUP)
            def _(o):
                copy(o).wait_send()

        return start, arrive, sent

    in_start, in_arrive, in_sent = exchange(0, x_ref, st.at[0])
    ct_start, ct_arrive, ct_sent = exchange(1, ct_ref, gst.at[SECTIONS])
    out_start, out_arrive, out_sent = exchange(2, st.at[SECTIONS], out_ref)
    gin_start, gin_arrive, gin_sent = exchange(3, gst.at[0], gin_ref)
    in_start()
    ct_start()

    acc_be[...] = jnp.zeros_like(acc_be)
    acc_br[...] = jnp.zeros_like(acc_br)
    acc_gg[...] = jnp.zeros_like(acc_gg)
    for load in small_loads:
        load.wait()
    sigma = jax.nn.sigmoid(gl_ref[...])

    load_we.wait()
    load_wr.wait()
    own_x.wait()
    in_arrive()

    def rows_of(s):
        return pl.ds(pl.multiple_of(s * 128, 128), 128)

    def share(kind, s):
        rows = rows_of(s)
        if kind == 0:
            src, dst = hid_t.at[:, rows], hid_s.at[:, rows]
        elif kind == 1:
            src, dst = norm_t.at[:, rows], norm_s.at[:, rows]
        elif kind == 2:
            cols = pl.ds(pl.multiple_of(256 * (1 - core), 256), 256)
            src, dst = gout.at[rows, cols], gout_s.at[rows]
        else:
            cols = pl.ds(pl.multiple_of(512 * (1 - core), 512), 512)
            src, dst = gpre.at[rows, cols], gpre_s.at[rows]
        return remote(src, dst, s_send.at[kind, s], s_recv.at[kind, s], sibling)

    def shared(kind):
        for s in range(SECTIONS):
            share(kind, s).wait_recv()

    def joined_of(s):
        lower = st[s, 0:8].reshape(128, 256).astype(F32)
        upper = st[s, 8:16].reshape(128, 256).astype(F32)
        return jnp.concatenate([lower, upper], axis=1)

    def forward(s):
        cols = pl.ds(pl.multiple_of(s * 128, 128), 128)
        joined = joined_of(s)
        centred = joined - jnp.mean(joined, axis=1, keepdims=True)
        inv_std = lax.rsqrt(jnp.mean(centred * centred, axis=1, keepdims=True) + EPSILON)
        normed = centred * inv_std
        nrm[s] = normed
        inv[s] = inv_std
        low = normed.astype(BF16)
        norm_t[:, cols] = low.T
        mixed = sigma * joined + br_ref[...]
        for h in range(4):
            hs = slice(256 * h, 256 * h + 256)
            pre = dot(low, we[:, hs], NN) + be_ref[:, hs]
            cdf = 0.5 + 0.5 * lax.erf(pre * math.sqrt(0.5))
            pdf = jnp.exp(-0.5 * pre * pre) * (1.0 / math.sqrt(2.0 * math.pi))
            dgelu[s, :, hs] = cdf + pre * pdf
            hidden = (pre * cdf).astype(BF16)
            hid_t[hs, cols] = hidden.T
            mixed = mixed + dot(hidden, wr[hs, :], NN)
        result = mixed.astype(BF16)
        for j in range(8):
            st[s + 1, 2 * j] = result[16 * j : 16 * j + 16, :256]
            st[s + 1, 2 * j + 1] = result[16 * j : 16 * j + 16, 256:]

    @pl.loop(0, SECTIONS)
    def _(s):
        forward(s)
        share(0, s).start()
        share(1, s).start()

    out_start()
    own_out = pltpu.make_async_copy(st.at[SECTIONS, member], out_ref.at[member], load_sem.at[4])
    own_out.start()

    own_ct.wait()
    ct_arrive()

    def upstream(s):
        lower = jnp.concatenate([gst[s + 1, 2 * j] for j in range(8)], axis=0)
        upper = jnp.concatenate([gst[s + 1, 2 * j + 1] for j in range(8)], axis=0)
        gout[rows_of(s), :] = jnp.concatenate([lower, upper], axis=1)

    def fold(v):
        return jnp.sum(v.reshape(16, 8, v.shape[1]), axis=0)

    def backward_hidden(s):
        grad = gout[rows_of(s), :]
        wide = grad.astype(F32)
        acc_br[...] += fold(wide)
        acc_gg[...] += fold(wide * joined_of(s))
        for h in range(4):
            hs = slice(256 * h, 256 * h + 256)
            pre = dot(grad, wr[hs, :], NT) * dgelu[s, :, hs]
            acc_be[:, hs] += fold(pre)
            gpre[rows_of(s), hs] = pre.astype(BF16)

    def backward_joined(s):
        wide = gout[rows_of(s), :].astype(F32)
        gnormed = dot(gpre[rows_of(s), :], we[...], NT)
        normed = nrm[s]
        mean = jnp.mean(gnormed, axis=1, keepdims=True)
        along = jnp.mean(gnormed * normed, axis=1, keepdims=True)
        result = (sigma * wide + inv[s] * (gnormed - mean - normed * along)).astype(BF16)
        gst[s, 0:8] = result[:, :256].reshape(8, 16, 256)
        gst[s, 8:16] = result[:, 256:].reshape(8, 16, 256)

    def product(k, hid, norm, grad, pre):
        if k < 2:
            return dot(hid[512 * k : 512 * k + 512, :], grad, NN)
        return dot(norm[...], pre, NN)

    def mine(k):
        grad = gout[:, pl.ds(pl.multiple_of(256 * core, 256), 256)] if k < 2 else None
        pre = gpre[:, pl.ds(pl.multiple_of(512 * core + 256 * (k - 2), 256), 256)] if k >= 2 else None
        return product(k, hid_t, norm_t, grad, pre)

    def begin(k):
        own[k] = mine(k)

    x_first = (True, False, True, False)

    def first(k, o):
        if x_first[k]:
            v = lax.rem(x + o, 4)
            src = part.at[k, v]
            device = at_x(v)
        else:
            v = lax.rem(y + o, 4)
            src = part.at[k, :, v]
            device = at_y(v)
        return remote(src, recv1.at[k, o], p_send.at[k, o], p_recv.at[k, o], device)

    def second(k, o):
        if x_first[k]:
            v = lax.rem(y + o, 4)
            device = at_y(v)
        else:
            v = lax.rem(x + o, 4)
            device = at_x(v)
        return remote(mid.at[k, v], recv2.at[k, o], q_send.at[k, o], q_recv.at[k, o], device)

    def scatter(k):
        grad = gout_s[...] if k < 2 else None
        pre = gpre_s[:, 256 * (k - 2) : 256 * (k - 1)] if k >= 2 else None
        total = (own[k] if k < 2 else mine(k)) + product(k, hid_s, norm_s, grad, pre)
        blocks = total.reshape((2, 16, 16, 256) if k < 2 else (4, 16, 8, 256))
        value = jnp.concatenate([blocks[i] for i in range(blocks.shape[0])], axis=1)
        part[k] = value.astype(BF16).reshape(4, 4, 32, 256)
        for o in (2, 1, 3):
            first(k, o).start()

    def scatter_again(k):
        for o in range(1, 4):
            first(k, o).wait_recv()
        mine = part[k, x] if x_first[k] else part[k, :, y]
        total = mine.astype(F32)
        for o in range(1, 4):
            total = total + recv1[k, o].astype(F32)
        mid[k] = total.astype(BF16)
        for o in (2, 1, 3):
            second(k, o).start()

    def reduced(k):
        for o in range(1, 4):
            second(k, o).wait_recv()
        total = (mid[k, y] if x_first[k] else mid[k, x]).astype(F32)
        for o in range(1, 4):
            total = total + recv2[k, o].astype(F32)
        return total

    def z_copy(half, o):
        v = lax.rem(z + o, 8)
        return remote(
            zsend.at[half, lax.rem(v, 4)], zrecv.at[half, z], z_send.at[half, o], z_recv.at[half, o], at_z(v)
        )

    def z_begin(half):
        for o in (4, 3, 5, 2, 6, 1, 7):
            z_copy(half, o).start()
        zrecv[half, z] = zsend[half, z_lo]

    def final_copy(half):
        return remote(fin.at[half], rfin.at[half], c_send.at[half], c_recv.at[half], sibling)

    def z_end(half):
        for o in range(1, 8):
            v = lax.rem(z + 8 - o, 8)
            remote(
                zsend.at[half, 0], zrecv.at[half, v], z_send.at[half, o], z_recv.at[half, o], at_z(v)
            ).wait_recv()
        total = zrecv[half, 0].astype(F32)
        for v in range(1, 8):
            total = total + zrecv[half, v].astype(F32)
        fin[half] = total * factor
        final_copy(half).start()

    def b_copy(n, o):
        sems = (b_send.at[n, o], b_recv.at[n, o])
        if n == 0:
            return remote(vec.at[1 - core], rvec, *sems, sibling)
        if n == 1:
            return remote(vx.at[x], vx.at[x], *sems, at_x(lax.rem(x + o, 4)))
        if n == 2:
            return remote(vy.at[y], vy.at[y], *sems, at_y(lax.rem(y + o, 4)))
        if n == 3:
            return remote(vz.at[z], vz.at[z], *sems, at_z(lax.rem(z + o, 8)))
        return remote(small.at[core], small.at[core], *sems, sibling)

    def b_arrive(n, o):
        sems = (b_send.at[n, o], b_recv.at[n, o])
        if n == 0:
            remote(vec.at[core], rvec, *sems, sibling).wait_recv()
        elif n == 1:
            v = lax.rem(x + 4 - o, 4)
            remote(vx.at[v], vx.at[v], *sems, at_x(v)).wait_recv()
        elif n == 2:
            v = lax.rem(y + 4 - o, 4)
            remote(vy.at[v], vy.at[v], *sems, at_y(v)).wait_recv()
        elif n == 3:
            v = lax.rem(z + 8 - o, 8)
            remote(vz.at[v], vz.at[v], *sems, at_z(v)).wait_recv()
        else:
            remote(small.at[1 - core], small.at[1 - core], *sems, sibling).wait_recv()

    B_COUNT = (range(0, 1), range(1, 4), range(1, 4), range(1, 8), range(0, 1))

    def b_begin(n):
        for o in B_COUNT[n]:
            b_copy(n, o).start()

    def b_end(n):
        for o in B_COUNT[n]:
            b_arrive(n, o)

    @pl.loop(0, SECTIONS - 1)
    def _(i):
        s = SECTIONS - 1 - i
        upstream(s)
        share(2, s).start()
        backward_hidden(s)
        share(3, s).start()
        backward_joined(s)

    def put(half, row, v):
        total = jnp.sum(v, axis=0, keepdims=True)
        for i in range(v.shape[1] // 128):
            vec[half, row + i : row + i + 1, :] = total[:, 128 * i : 128 * i + 128]

    upstream(0)
    share(2, 0).start()
    backward_hidden(0)
    share(3, 0).start()
    begin(0)
    begin(1)
    put(0, 0, acc_be[...])
    put(1, 0, acc_br[...])
    put(1, 4, acc_gg[...])
    b_begin(0)
    shared(0)
    shared(2)
    scatter(0)
    scatter(1)
    b_end(0)
    vx[x] = vec[core] + rvec[...]
    b_begin(1)
    shared(1)
    shared(3)
    scatter(2)
    scatter(3)
    backward_joined(0)
    in_sent()
    ct_sent()
    out_sent()
    own_out.wait()
    out_arrive()
    scatter_again(0)
    scatter_again(1)
    b_end(1)
    vy[y] = (vx[0] + vx[1]) + (vx[2] + vx[3])
    b_begin(2)
    scatter_again(2)
    scatter_again(3)
    gin_start()
    own_gin = pltpu.make_async_copy(gst.at[0, member], gin_ref.at[member], load_sem.at[5])
    own_gin.start()
    for k in range(2):
        block = reduced(k)
        for i in range(2):
            zsend[0, 2 * k + i] = block[16 * i : 16 * i + 16].astype(BF16)
    z_begin(0)
    b_end(2)
    vz[z] = (vy[0] + vy[1]) + (vy[2] + vy[3])
    b_begin(3)
    left = reduced(2)
    right = reduced(3)
    for i in range(4):
        rows = slice(8 * i, 8 * i + 8)
        zsend[1, i] = jnp.concatenate([left[rows], right[rows]], axis=0).astype(BF16)
    z_begin(1)
    z_end(0)
    b_end(3)
    total = vz[0]
    for v in range(1, 8):
        total = total + vz[v]
    small[core] = total * factor
    b_begin(4)
    own_gin.wait()
    gin_arrive()
    gin_sent()
    for k in range(4):
        for i in range(SECTIONS):
            share(k, i).wait_send()
        for o in range(1, 4):
            first(k, o).wait_send()
            second(k, o).wait_send()
    z_end(1)

    def place(half, value, who):
        if half == 0:
            o_wr[:, pl.ds(pl.multiple_of(256 * who, 256), 256)] = value
        else:
            for i in range(2):
                o_we[:, pl.ds(pl.multiple_of(512 * who + 256 * i, 256), 256)] = value[8 * i : 8 * i + 8]

    for half in range(2):
        place(half, fin[half], core)
    for half in range(2):
        final_copy(half).wait_recv()
        place(half, rfin[half], 1 - core)
    b_end(4)
    for i in range(8):
        o_be[:, 128 * i : 128 * i + 128] = small[0, i : i + 1]
    for i in range(4):
        cols = slice(128 * i, 128 * i + 128)
        o_br[:, cols] = small[1, i : i + 1]
        sg = sigma[:, cols]
        o_gg[:, cols] = small[1, 4 + i : 5 + i] * (sg * (1.0 - sg))

    for half in range(2):
        final_copy(half).wait_send()
        for o in range(1, 8):
            z_copy(half, o).wait_send()
    for n in range(5):
        for o in B_COUNT[n]:
            b_copy(n, o).wait_send()


def finish(*refs):
    n = len(refs) // 2
    copies = [pltpu.make_async_copy(refs[i], refs[n + i], refs[2 * n].at[i]) for i in range(n)]
    for copy in copies:
        copy.start()
    for copy in copies:
        copy.wait()


def hand_on(arrays):
    n = len(arrays)
    return pl.pallas_call(
        finish,
        out_shape=tuple(jax.ShapeDtypeStruct(a.shape, a.dtype) for a in arrays),
        in_specs=[pl.BlockSpec(memory_space=pl.ANY)] * n,
        out_specs=(pl.BlockSpec(memory_space=pltpu.HBM),) * n,
        scratch_shapes=[pltpu.SemaphoreType.DMA((n,))],
        compiler_params=pltpu.CompilerParams(vmem_limit_bytes=1024 * 1024),
    )(*arrays)


def body(inputs, w_expand, b_expand, w_reduce, b_reduce, gate_logit, cotangent):
    rows, width = inputs.shape[1:]
    hidden = w_expand.shape[1]
    block = rows // GROUP
    factor = 1.0 / math.sqrt(lax.axis_size("rep") * lax.axis_size("ctx") * rows)
    any_spec = pl.BlockSpec(memory_space=pl.ANY)
    vmem = pl.BlockSpec(memory_space=pltpu.VMEM)
    dma = pltpu.SemaphoreType.DMA
    results = pl.pallas_call(
        functools.partial(kernel, factor),
        out_shape=(
            jax.ShapeDtypeStruct((GROUP, block, width), BF16),
            jax.ShapeDtypeStruct((GROUP, block, width), BF16),
            jax.ShapeDtypeStruct((8, 1024), F32),
            jax.ShapeDtypeStruct((1, 1024), F32),
            jax.ShapeDtypeStruct((16, 512), F32),
            jax.ShapeDtypeStruct((1, 512), F32),
            jax.ShapeDtypeStruct((1, 512), F32),
        ),
        in_specs=[pl.BlockSpec(memory_space=pltpu.HBM)] * 7,
        out_specs=(any_spec, any_spec, vmem, vmem, vmem, vmem, vmem),
        scratch_shapes=[
            pltpu.VMEM((512, 1024), BF16),
            pltpu.VMEM((1024, 512), BF16),
            pltpu.VMEM((1, 1024), F32),
            pltpu.VMEM((1, 512), F32),
            pltpu.VMEM((1, 512), F32),
            pltpu.VMEM((SECTIONS + 1, 16, 16, 256), BF16),
            pltpu.VMEM((SECTIONS + 1, 16, 16, 256), BF16),
            pltpu.VMEM((SECTIONS, 128, 512), F32),
            pltpu.VMEM((SECTIONS, 128, 1), F32),
            pltpu.VMEM((512, 512), BF16),
            pltpu.VMEM((1024, 512), BF16),
            pltpu.VMEM((SECTIONS, 128, 1024), F32),
            pltpu.VMEM((512, 512), BF16),
            pltpu.VMEM((512, 1024), BF16),
            pltpu.VMEM((1024, 512), BF16),
            pltpu.VMEM((512, 512), BF16),
            pltpu.VMEM((512, 256), BF16),
            pltpu.VMEM((512, 512), BF16),
            pltpu.VMEM((2, 512, 256), F32),
            pltpu.VMEM((4, 4, 4, 32, 256), BF16),
            pltpu.VMEM((4, 4, 4, 32, 256), BF16),
            pltpu.VMEM((4, 4, 32, 256), BF16),
            pltpu.VMEM((4, 4, 32, 256), BF16),
            pltpu.VMEM((2, 4, 16, 256), BF16),
            pltpu.VMEM((2, 8, 16, 256), BF16),
            pltpu.VMEM((2, 16, 256), F32),
            pltpu.VMEM((2, 16, 256), F32),
            pltpu.VMEM((8, 1024), F32),
            pltpu.VMEM((8, 512), F32),
            pltpu.VMEM((8, 512), F32),
            pltpu.VMEM((2, 8, 128), F32),
            pltpu.VMEM((8, 128), F32),
            pltpu.VMEM((4, 8, 128), F32),
            pltpu.VMEM((4, 8, 128), F32),
            pltpu.VMEM((8, 8, 128), F32),
            pltpu.VMEM((2, 8, 128), F32),
            dma((9,)),
            dma((4, 16)),
            dma((4, 16)),
            dma((2,)),
            dma((2,)),
            dma((4, SECTIONS)),
            dma((4, SECTIONS)),
            dma((4, 4)),
            dma((4, 4)),
            dma((4, 4)),
            dma((4, 4)),
            dma((2, 8)),
            dma((2, 8)),
            dma((5, 8)),
            dma((5, 8)),
        ],
        compiler_params=pltpu.CompilerParams(collective_id=0, has_side_effects=True, vmem_limit_bytes=24 * 1024 * 1024),
    )(
        *(
            pltpu.with_memory_space_constraint(value, pltpu.HBM)
            for value in (
                inputs.reshape(GROUP, block, width),
                w_expand,
                b_expand.reshape(1, hidden),
                w_reduce,
                b_reduce.reshape(1, 2 * width),
                gate_logit.reshape(1, 2 * width),
                cotangent.reshape(GROUP, block, width),
            )
        )
    )
    out, gin, g_we, g_be, g_wr, g_br, g_gg = hand_on(results)
    return (
        out.reshape(inputs.shape),
        gin.reshape(inputs.shape),
        g_we,
        g_be.reshape(hidden),
        g_wr,
        g_br.reshape(2 * width),
        g_gg.reshape(2 * width),
    )


def solution(mesh):
    return jax.shard_map(
        body,
        mesh=mesh,
        in_specs=(P("rep", "ctx", None), P(), P(), P(), P(), P(), P("rep", "ctx", None)),
        out_specs=(
            P("rep", "ctx", None),
            P("rep", "ctx", None),
            P("ctx", None),
            P(),
            P("ctx", None),
            P(),
            P(),
        ),
        check_vma=False,
    )
```
